512 devices in a mesh: drop: 16 (over z, core), freq: 32 (over x, y).
Axes of the slice: x: 4, y: 8, z: 8, core: 2. Of those that a mesh axis runs over, the one named last changes fastest.
Arguments:
- taps: float32 [32, 2, 23, 128], P('drop', None, None, 'freq'), may hold values from -6 to 6
- echo_lags: int32 [32, 23], P('drop'), may hold values from 0 to 319
- front_gain: float32 [4096], P('freq'), may hold values from 0.35 to 2, as said below
- symbols: int32 [32, 16, 4, 4096], P('drop', None, None, 'freq'), may hold values from 0 to 15
- noise: bfloat16 [32, 16, 2, 32, 4096], P('drop', None, None, None, 'freq'), may hold values from -6 to 6
- noise_std: float32 [32, 16], P('drop'), may hold values from 0.15 to 1.5
Outputs:
- detected: bfloat16 [32, 16, 2, 4, 4096], P('drop', None, None, None, 'freq')
- error_power: float32 [16], replicated
The draws below stay inside these ranges and needn't reach their ends.
Inputs may be any that keep to these rules, and one draw needn't show every extreme that they name: `symbols`: 16-QAM indices. `front_gain`: positive front end amplitudes.
All inputs are finite; a program needn't handle non-finite values.
Results may differ from the reference program's by a relative error of at most 0.001.
Values sent between devices are 32-bit elements; how exact they have to be, the bound alone decides.
A program may use at most 64 MiB of HBM per device.

```python
import math
import jax
import jax.numpy as jnp
from jax import lax

RX = 32
TX = 4
TAPS = 23
FOURIER_POINTS = 4096
SNRS = 16
MAXD = 320
DROPS = 32
LINKS = 128


def draw_front_gain(key, part):
    tone_positions = jnp.arange(FOURIER_POINTS, dtype=jnp.float32)
    rotation_rate = tone_positions / (FOURIER_POINTS - 1) - 0.5
    tilted = jnp.exp(0.5 * math.log(3.0) * rotation_rate)
    rough = jax.random.uniform(key, (FOURIER_POINTS,), jnp.float32, 0.7, 1.4)
    return (tilted * rough).astype(jnp.float32)


def with_ends(result, rng, least, largest):
    index_at = [jax.random.randint(jax.random.fold_in(rng, axis), (), 0, length) for axis, length in enumerate(result.shape)]
    main_axis = result.shape.index(max(result.shape))
    next_to = index_at[:main_axis] + [(index_at[main_axis] + 1) % result.shape[main_axis]] + index_at[main_axis + 1:]
    return result.at[tuple(index_at)].set(least).at[tuple(next_to)].set(largest)


def steps_of(rng, dims, cuts, least, high):
    loudness, own = 1.0, jax.random.fold_in(rng, 6)
    for dim, blocks in cuts:
        draws = jnp.exp(jax.random.uniform(jax.random.fold_in(own, dim), (blocks,), jnp.float32, least / len(cuts), high / len(cuts)))
        loudness = loudness * jnp.repeat(draws, dims[dim] // blocks).reshape([-1 if axis == dim else 1 for axis in range(len(dims))])
    return loudness


def scatter_about(rng, dims, scale, bound, shards=(), kind=jnp.bfloat16):
    result = scale * jax.random.normal(rng, dims, jnp.float32)
    if shards:
        result = result * steps_of(rng, dims, shards, -0.22, 0.18)
    return jnp.clip(result, -bound, bound).astype(kind)


def setup_inputs(seed: int = 0) -> dict:
    seeds = jax.random.split(jax.random.key(seed), 7)
    return {
        "taps": scatter_about(seeds[0], (DROPS, 2, TAPS, LINKS), 1.0, 6.0, ((0, 16), (3, 32)), jnp.float32),
        "echo_lags": with_ends(jax.random.randint(seeds[1], (DROPS, TAPS), 0, MAXD), jax.random.fold_in(seeds[1], 1), 0, MAXD - 1).astype(jnp.int32),
        "front_gain": draw_front_gain(jax.random.fold_in(seeds[6], 71), 0),
        "symbols": with_ends(jax.random.randint(seeds[3], (DROPS, SNRS, TX, FOURIER_POINTS), 0, 16), jax.random.fold_in(seeds[3], 1), 0, 15).astype(jnp.int32),
        "noise": scatter_about(seeds[4], (DROPS, SNRS, 2, RX, FOURIER_POINTS), 1.0, 6.0, ((0, 16), (4, 32))),
        "noise_std": jnp.clip(jnp.exp(math.log(1.5) - 2.3025851 * jax.random.uniform(seeds[5], (DROPS, SNRS), jnp.float32) ** steps_of(seeds[5], (DROPS, SNRS), ((0, 16),), -0.2, 0.2)), 0.15, 1.5),
    }


level_scale = 1.0 / math.sqrt(10.0)

def complex_mul(left_re, left_im, right_re, right_im):
    return (left_re * right_re - left_im * right_im, left_re * right_im + left_im * right_re)

def solve_small(gram_re, gram_im, rhs_re, rhs_im):
    streams = len(rhs_re)
    gram_re = [list(row) for row in gram_re]
    gram_im = [list(row) for row in gram_im]
    rhs_re = list(rhs_re)
    rhs_im = list(rhs_im)
    inverse = []
    for i in range(streams):
        pivot_inv = 1.0 / gram_re[i][i]
        inverse.append(pivot_inv)
        for j in range(i + 1, streams):
            factor_re = gram_re[j][i] * pivot_inv
            factor_im = gram_im[j][i] * pivot_inv
            for k in range(i + 1, streams):
                prod_re, prod_im = complex_mul(factor_re, factor_im, gram_re[i][k], gram_im[i][k])
                gram_re[j][k] = gram_re[j][k] - prod_re
                gram_im[j][k] = gram_im[j][k] - prod_im
            prod_re, prod_im = complex_mul(factor_re, factor_im, rhs_re[i], rhs_im[i])
            rhs_re[j] = rhs_re[j] - prod_re
            rhs_im[j] = rhs_im[j] - prod_im
    result_re = [None] * streams
    result_im = [None] * streams
    for i in reversed(range(streams)):
        partial_re, partial_im = (rhs_re[i], rhs_im[i])
        for k in range(i + 1, streams):
            prod_re, prod_im = complex_mul(gram_re[i][k], gram_im[i][k], result_re[k], result_im[k])
            partial_re = partial_re - prod_re
            partial_im = partial_im - prod_im
        result_re[i] = partial_re * inverse[i]
        result_im[i] = partial_im * inverse[i]
    return (result_re, result_im)

def one_drop(items, front_gain):
    tap_pair, echo_lag, symbol, noise, noise_std = items
    highest = lax.Precision.HIGHEST
    tone_positions = jnp.arange(FOURIER_POINTS, dtype=jnp.int32)
    rotation_cycles = echo_lag[:, None] * tone_positions[None, :] % FOURIER_POINTS
    angle = rotation_cycles.astype(jnp.float32) * (2.0 * math.pi / FOURIER_POINTS)
    cosine = jnp.cos(angle)
    sine = jnp.sin(angle)
    resp_re = jnp.dot(tap_pair[0].T, cosine, precision=highest) + jnp.dot(tap_pair[1].T, sine, precision=highest)
    resp_im = jnp.dot(tap_pair[1].T, cosine, precision=highest) - jnp.dot(tap_pair[0].T, sine, precision=highest)
    resp_re = resp_re * front_gain[None, :]
    resp_im = resp_im * front_gain[None, :]
    power = jnp.sum(resp_re * resp_re + resp_im * resp_im) / (FOURIER_POINTS * RX * TX)
    scaling = 1.0 / jnp.sqrt(power)
    chan_re = (resp_re * scaling).reshape(RX, TX, FOURIER_POINTS)
    chan_im = (resp_im * scaling).reshape(RX, TX, FOURIER_POINTS)
    sent_re = (2 * (symbol % 4) - 3).astype(jnp.float32) * level_scale
    sent_im = (2 * (symbol // 4) - 3).astype(jnp.float32) * level_scale
    noise_re = noise[:, 0].astype(jnp.float32)
    noise_im = noise[:, 1].astype(jnp.float32)
    spread = noise_std[:, None, None]
    recv_re = spread * noise_re
    recv_im = spread * noise_im
    for t in range(TX):
        recv_re = recv_re + chan_re[None, :, t] * sent_re[:, None, t] - chan_im[None, :, t] * sent_im[:, None, t]
        recv_im = recv_im + chan_re[None, :, t] * sent_im[:, None, t] + chan_im[None, :, t] * sent_re[:, None, t]
    gram_re = jnp.einsum('rtk,ruk->tuk', chan_re, chan_re, precision=highest) + jnp.einsum('rtk,ruk->tuk', chan_im, chan_im, precision=highest)
    gram_im = jnp.einsum('rtk,ruk->tuk', chan_re, chan_im, precision=highest) - jnp.einsum('rtk,ruk->tuk', chan_im, chan_re, precision=highest)
    match_re = jnp.einsum('rtk,srk->stk', chan_re, recv_re, precision=highest) + jnp.einsum('rtk,srk->stk', chan_im, recv_im, precision=highest)
    match_im = jnp.einsum('rtk,srk->stk', chan_re, recv_im, precision=highest) - jnp.einsum('rtk,srk->stk', chan_im, recv_re, precision=highest)
    entries_re = [[gram_re[t, u][None, :] for u in range(TX)] for t in range(TX)]
    entries_im = [[gram_im[t, u][None, :] for u in range(TX)] for t in range(TX)]
    result_re, result_im = solve_small(entries_re, entries_im, [match_re[:, t] for t in range(TX)], [match_im[:, t] for t in range(TX)])
    estimate_re = jnp.stack(result_re, 1)
    estimate_im = jnp.stack(result_im, 1)
    squared = (estimate_re - sent_re) ** 2 + (estimate_im - sent_im) ** 2
    errors = lax.optimization_barrier(jnp.sum(squared, axis=(1, 2)))
    detected = jnp.stack([estimate_re, estimate_im], 1).astype(jnp.bfloat16)
    return (detected, errors)

def reference(taps, echo_lags, front_gain, symbols, noise, noise_std):
    detected, errors = lax.map(lambda items: one_drop(items, front_gain), (taps, echo_lags, symbols, noise, noise_std))
    drops_all = taps.shape[0]
    error_power = RX * lax.optimization_barrier(jnp.sum(errors, axis=0)) / (drops_all * TX * FOURIER_POINTS)
    return (detected, error_power)
```

```python
import math

import jax
import jax.numpy as jnp
from jax import lax
from jax.experimental import pallas as pl
from jax.experimental.pallas import tpu as pltpu
from jax.sharding import PartitionSpec as P

RX = 32
TX = 4
TAPS = 23
SNRS = 16
FOURIER_POINTS = 4096
DROPS = 32
LANES = 128
MESH = pl.DeviceIdType.MESH
F32 = jnp.float32

level_scale = 1.0 / math.sqrt(10.0)


def cos_sin(cycles):
    shifted = cycles + 512
    quadrant = lax.shift_right_logical(shifted, 10) & 3
    x = ((shifted & 1023) - 512).astype(F32) * (2.0 * math.pi / FOURIER_POINTS)
    x2 = x * x
    s = x * (1.0 + x2 * (-1 / 6 + x2 * (1 / 120 + x2 * (-1 / 5040 + x2 * (1 / 362880)))))
    c = 1.0 + x2 * (-0.5 + x2 * (1 / 24 + x2 * (-1 / 720 + x2 * (1 / 40320 + x2 * (-1 / 3628800)))))
    odd = (quadrant & 1) == 1
    cosine = jnp.where(odd, s, c)
    sine = jnp.where(odd, c, s)
    cosine = jnp.where((quadrant == 1) | (quadrant == 2), -cosine, cosine)
    sine = jnp.where(quadrant >= 2, -sine, sine)
    return cosine, sine


def over_sublanes(x):
    x = (x[0:8] + x[8:16]) + (x[16:24] + x[24:32])
    x = x + pltpu.roll(x, 4, 0)
    x = x + pltpu.roll(x, 2, 0)
    return x + pltpu.roll(x, 1, 0)


def cmul(a, b):
    return a[0] * b[0] - a[1] * b[1], a[0] * b[1] + a[1] * b[0]


def cmul_conj(a, b):
    return a[0] * b[0] + a[1] * b[1], a[0] * b[1] - a[1] * b[0]


def csub(a, b):
    return a[0] - b[0], a[1] - b[1]


def kernel(
    taps_hbm, lags_hbm, gain_hbm, symbols_hbm, noise_hbm, std_hbm,
    detected_ref, error_ref,
    taps_v, lags_v, gain_v, symbols_v, noise_v, std_v,
    packed, padded, column, gathered, table, channel, noise_f, out_f, row_send, rows, sum_send, sums,
    in_sems, send_sems, recv_sems,
):
    n_freq, n_drop = lax.axis_size("freq"), lax.axis_size("drop")
    freq, drop = lax.axis_index("freq"), lax.axis_index("drop")
    barrier = pltpu.get_barrier_semaphore()

    def freq_peer(i):
        return {"freq": lax.rem(freq + i, n_freq)}

    def drop_peer(i):
        return {"drop": lax.rem(drop + i, n_drop)}

    @pl.loop(1, n_freq)
    def _(i):
        pl.semaphore_signal(barrier, inc=1, device_id=freq_peer(i), device_id_type=MESH)

    @pl.loop(1, n_drop)
    def _(i):
        pl.semaphore_signal(barrier, inc=1, device_id=drop_peer(i), device_id_type=MESH)

    loads = [
        pltpu.make_async_copy(src, dst, in_sems.at[i])
        for i, (src, dst) in enumerate(
            (
                (taps_hbm, taps_v), (lags_hbm, lags_v), (gain_hbm, gain_v),
                (symbols_hbm, symbols_v), (noise_hbm, noise_v), (std_hbm, std_v),
            )
        )
    ]
    for load in loads:
        load.start()

    padded[...] = jnp.zeros_like(padded)
    loads[0].wait()
    for q in range(4):
        padded[q, :, 0:TAPS] = taps_v[q // 2, q % 2]
    own = padded[0]
    for q in range(1, 4):
        own = own + pltpu.roll(padded[q], 32 * q, 1)
    packed[...] = own
    gathered[freq] = own

    pl.semaphore_wait(barrier, n_freq + n_drop - 2)

    def send_taps(i):
        return pltpu.make_async_remote_copy(
            src_ref=packed, dst_ref=gathered.at[freq], send_sem=send_sems.at[0], recv_sem=recv_sems.at[0],
            device_id=freq_peer(i), device_id_type=MESH,
        )

    @pl.loop(1, n_freq)
    def _(i):
        send_taps(i).start()

    loads[1].wait()
    loads[2].wait()
    loads[5].wait()
    column[...] = jnp.zeros_like(column)
    column[0:2, 0:TAPS] = lags_v[...].astype(F32)
    column[2:4, 0:SNRS] = std_v[...]
    turned = jnp.transpose(column[...])
    gain = gain_v[...]
    tone = freq * LANES + lax.broadcasted_iota(jnp.int32, (32, LANES), 1)
    table[...] = jnp.zeros_like(table)
    for d in range(2):
        lag = turned[0:32, d : d + 1].astype(jnp.int32)
        cosine, sine = cos_sin((lag * tone) & (FOURIER_POINTS - 1))
        cosine = cosine * gain
        sine = sine * gain
        table[64 * d : 64 * d + 32, 256 * d : 256 * d + 128] = cosine
        table[64 * d + 32 : 64 * d + 64, 256 * d : 256 * d + 128] = sine
        table[64 * d : 64 * d + 32, 256 * d + 128 : 256 * d + 256] = -sine
        table[64 * d + 32 : 64 * d + 64, 256 * d + 128 : 256 * d + 256] = cosine
    std = [jnp.broadcast_to(turned[0:SNRS, 2 + d : 3 + d], (SNRS, LANES)).reshape(2, 8, LANES) for d in range(2)]

    loads[4].wait()

    @pl.loop(0, 32)
    def _(i):
        at = pl.ds(pl.multiple_of(i * 64, 64), 64)
        noise_f[at, :] = noise_v[at, :].astype(F32)

    pltpu.make_async_remote_copy(
        src_ref=gathered.at[pl.ds(0, n_freq - 1)], dst_ref=gathered.at[pl.ds(0, n_freq - 1)],
        send_sem=send_sems.at[0], recv_sem=recv_sems.at[0], device_id=freq_peer(1), device_id_type=MESH,
    ).wait_recv()
    response = jnp.dot(
        gathered[...].reshape(RX * TX, LANES), table[...],
        precision=lax.Precision.HIGHEST, preferred_element_type=F32,
    )
    for q in range(4):
        channel[q] = response[:, LANES * q : LANES * (q + 1)]

    def match_step(r, so_far):
        result = []
        for d in range(2):
            noise = [noise_f[pl.ds(1024 * d + 32 * c + r, SNRS, stride=64), :].reshape(2, 8, LANES) for c in range(2)]
            for t in range(TX):
                h = [channel[2 * d + c, pl.ds(TX * r + t, 1), :] for c in range(2)]
                h = [jnp.broadcast_to(v, (8, LANES))[None] for v in h]
                re, im = cmul_conj(h, noise)
                old_re, old_im = so_far[4 * d + t]
                result.append((old_re + re, old_im + im))
        return tuple(result)

    nothing = jnp.zeros((2, 8, LANES), F32)
    match = lax.fori_loop(0, RX, match_step, ((nothing, nothing),) * 8, unroll=4)

    solved, totals, powers = [], [], []
    for d in range(2):
        h = [[channel[2 * d + c, pl.ds(t, RX, stride=TX), :] for c in range(2)] for t in range(TX)]
        diagonal = [over_sublanes(h[t][0] * h[t][0] + h[t][1] * h[t][1]) for t in range(TX)]
        upper = {}
        for t in range(TX):
            for u in range(t + 1, TX):
                re, im = cmul_conj(h[t], h[u])
                upper[t, u] = over_sublanes(re), over_sublanes(im)
        powers.append((diagonal[0] + diagonal[1]) + (diagonal[2] + diagonal[3]))
        right = [match[4 * d + t] for t in range(TX)]
        inverse = []
        for i in range(TX):
            inverse.append(1.0 / diagonal[i])
            for j in range(i + 1, TX):
                factor = upper[i, j][0] * inverse[i], -upper[i, j][1] * inverse[i]
                diagonal[j] = diagonal[j] - (factor[0] * upper[i, j][0] - factor[1] * upper[i, j][1])
                for k in range(j + 1, TX):
                    upper[j, k] = csub(upper[j, k], cmul(factor, upper[i, k]))
                right[j] = csub(right[j], cmul(factor, right[i]))
        result = [None] * TX
        for i in reversed(range(TX)):
            partial = right[i]
            for k in range(i + 1, TX):
                partial = csub(partial, cmul(upper[i, k], result[k]))
            result[i] = partial[0] * inverse[i], partial[1] * inverse[i]
        solved.append(result)
        total = result[0][0] * result[0][0] + result[0][1] * result[0][1]
        for t in range(1, TX):
            total = total + result[t][0] * result[t][0] + result[t][1] * result[t][1]
        totals.append(total * (std[d] * std[d]))

    lane8 = lax.broadcasted_iota(jnp.int32, (8, LANES), 1)
    sub8 = lax.broadcasted_iota(jnp.int32, (8, LANES), 0)
    power_rows = jnp.where(sub8 == 0, powers[0], jnp.where(sub8 == 1, powers[1], 0.0))
    stacked = [totals[0][0], totals[0][1], totals[1][0], totals[1][1], power_rows]
    row = jnp.zeros((8, LANES), F32)
    for i, piece in enumerate(stacked):
        row = row + jnp.where(lane8 == sub8 + 8 * i, jnp.sum(piece, axis=1, keepdims=True), 0.0)
    row = jnp.sum(row, axis=0, keepdims=True)
    row_send[...] = row
    rows[freq] = row

    def send_row(i):
        return pltpu.make_async_remote_copy(
            src_ref=row_send, dst_ref=rows.at[freq], send_sem=send_sems.at[1], recv_sem=recv_sems.at[1],
            device_id=freq_peer(i), device_id_type=MESH,
        )

    @pl.loop(1, n_freq)
    def _(i):
        send_row(i).start()

    loads[3].wait()
    sent = []
    for d in range(2):
        for t in range(TX):
            symbol = symbols_v[pl.ds(64 * d + t, SNRS, stride=TX), :]
            sent.append(
                (
                    (2 * (symbol & 3) - 3).astype(F32) * level_scale,
                    (2 * lax.shift_right_logical(symbol, 2) - 3).astype(F32) * level_scale,
                )
            )

    def all_rows(ref, n, i):
        pltpu.make_async_remote_copy(
            src_ref=ref.at[pl.ds(0, n - 1)], dst_ref=ref.at[pl.ds(0, n - 1)],
            send_sem=send_sems.at[i], recv_sem=recv_sems.at[i], device_id=freq_peer(1), device_id_type=MESH,
        ).wait_recv()
        return jnp.sum(ref[...], axis=0)

    row = all_rows(rows, n_freq, 1)
    lane = lax.broadcasted_iota(jnp.int32, (1, LANES), 1)
    power = [
        jnp.sum(jnp.where(lane == 32 + d, row, 0.0), axis=1, keepdims=True) * (1.0 / (FOURIER_POINTS * RX * TX))
        for d in range(2)
    ]
    weighted = row * jnp.where(lane < SNRS, power[0], jnp.where(lane < 2 * SNRS, power[1], 0.0))
    sum_send[...] = weighted
    sums[drop] = weighted

    def send_sum(i):
        return pltpu.make_async_remote_copy(
            src_ref=sum_send, dst_ref=sums.at[drop], send_sem=send_sems.at[2], recv_sem=recv_sems.at[2],
            device_id=drop_peer(i), device_id_type=MESH,
        )

    @pl.loop(1, n_drop)
    def _(i):
        send_sum(i).start()

    for d in range(2):
        amplitude = std[d] * jnp.sqrt(jnp.broadcast_to(power[d], (8, LANES)))
        for t in range(TX):
            for c in range(2):
                estimate = sent[4 * d + t][c] + (amplitude * solved[d][t][c]).reshape(SNRS, LANES)
                out_f[pl.ds(128 * d + 4 * c + t, SNRS, stride=8), :] = estimate
    detected_ref[...] = out_f[...].astype(jnp.bfloat16)

    total = all_rows(sums, n_drop, 2)
    total = total[:, 0:SNRS] + total[:, SNRS : 2 * SNRS]
    error_ref[...] = RX * total / (DROPS * TX * FOURIER_POINTS)

    for i, (ref, n) in enumerate(((gathered, n_freq), (rows, n_freq), (sums, n_drop))):
        pltpu.make_async_remote_copy(
            src_ref=ref.at[pl.ds(0, n - 1)], dst_ref=ref.at[pl.ds(0, n - 1)],
            send_sem=send_sems.at[i], recv_sem=recv_sems.at[i], device_id=freq_peer(1), device_id_type=MESH,
        ).wait_send()


def shards(taps, echo_lags, front_gain, symbols, noise, noise_std):
    n_freq, n_drop = lax.axis_size("freq"), lax.axis_size("drop")
    vmem = pltpu.VMEM
    detected, error = pl.pallas_call(
        kernel,
        out_shape=(
            jax.ShapeDtypeStruct((2 * SNRS * 8, LANES), jnp.bfloat16),
            jax.ShapeDtypeStruct((1, SNRS), F32),
        ),
        in_specs=[pl.BlockSpec(memory_space=pltpu.HBM)] * 6,
        out_specs=(pl.BlockSpec(memory_space=pltpu.VMEM), pl.BlockSpec(memory_space=pltpu.VMEM)),
        scratch_shapes=[
            vmem((2, 2, TX, TAPS), F32),
            vmem((2, TAPS), jnp.int32),
            vmem((1, LANES), F32),
            vmem((2 * SNRS * TX, LANES), jnp.int32),
            vmem((2 * SNRS * 2 * RX, LANES), jnp.bfloat16),
            vmem((2, SNRS), F32),
            vmem((TX, LANES), F32),
            vmem((4, TX, LANES), F32),
            vmem((LANES, LANES), F32),
            vmem((n_freq, TX, LANES), F32),
            vmem((LANES, 4 * LANES), F32),
            vmem((4, RX * TX, LANES), F32),
            vmem((2 * SNRS * 2 * RX, LANES), F32),
            vmem((2 * SNRS * 8, LANES), F32),
            vmem((1, LANES), F32),
            vmem((n_freq, 1, LANES), F32),
            vmem((1, LANES), F32),
            vmem((n_drop, 1, LANES), F32),
            pltpu.SemaphoreType.DMA((6,)),
            pltpu.SemaphoreType.DMA((3,)),
            pltpu.SemaphoreType.DMA((3,)),
        ],
        compiler_params=pltpu.CompilerParams(collective_id=0, has_side_effects=True),
    )(
        jnp.transpose(taps, (0, 1, 3, 2)),
        echo_lags,
        front_gain.reshape(1, LANES),
        symbols.reshape(2 * SNRS * TX, LANES),
        noise.reshape(2 * SNRS * 2 * RX, LANES),
        noise_std,
    )
    return detected.reshape(2, SNRS, 2, TX, LANES), error.reshape(SNRS)


def solution(mesh):
    placed = (
        P("drop", None, None, "freq"),
        P("drop", None),
        P("freq"),
        P("drop", None, None, "freq"),
        P("drop", None, None, None, "freq"),
        P("drop", None),
    )
    return jax.shard_map(
        shards,
        mesh=mesh,
        in_specs=placed,
        out_specs=(P("drop", None, None, None, "freq"), P()),
        check_vma=False,
    )
```

```python
import math

import jax
import jax.numpy as jnp
from jax import lax
from jax.experimental import pallas as pl
from jax.experimental.pallas import tpu as pltpu
from jax.sharding import PartitionSpec as P

RX = 32
TX = 4
TAPS = 23
SNRS = 16
FOURIER_POINTS = 4096
DROPS = 32
LANES = 128
NX, NY = 4, 8
ALONG_X = ((2, 0), (1, 0), (3, 0))
ALONG_Y = ((0, 4), (0, 3), (0, 5), (0, 2), (0, 6), (0, 1), (0, 7))
MESH = pl.DeviceIdType.MESH
F32 = jnp.float32

level_scale = 1.0 / math.sqrt(10.0)


def cos_sin(cycles):
    shifted = cycles + 512
    quadrant = lax.shift_right_logical(shifted, 10) & 3
    x = ((shifted & 1023) - 512).astype(F32) * (2.0 * math.pi / FOURIER_POINTS)
    x2 = x * x
    s = x * (1.0 + x2 * (-1 / 6 + x2 * (1 / 120 + x2 * (-1 / 5040 + x2 * (1 / 362880)))))
    c = 1.0 + x2 * (-0.5 + x2 * (1 / 24 + x2 * (-1 / 720 + x2 * (1 / 40320 + x2 * (-1 / 3628800)))))
    odd = (quadrant & 1) == 1
    cosine = jnp.where(odd, s, c)
    sine = jnp.where(odd, c, s)
    cosine = jnp.where((quadrant == 1) | (quadrant == 2), -cosine, cosine)
    sine = jnp.where(quadrant >= 2, -sine, sine)
    return cosine, sine


def over_sublanes(x):
    x = (x[0:8] + x[8:16]) + (x[16:24] + x[24:32])
    x = x + pltpu.roll(x, 4, 0)
    x = x + pltpu.roll(x, 2, 0)
    return x + pltpu.roll(x, 1, 0)


def cmul(a, b):
    return a[0] * b[0] - a[1] * b[1], a[0] * b[1] + a[1] * b[0]


def cmul_conj(a, b):
    return a[0] * b[0] + a[1] * b[1], a[0] * b[1] - a[1] * b[0]


def csub(a, b):
    return a[0] - b[0], a[1] - b[1]


def kernel(
    taps_hbm, lags_hbm, gain_hbm, symbols_hbm, noise_hbm, std_hbm,
    detected_ref, error_ref,
    taps_v, lags_v, gain_v, symbols_v, noise_v, std_v,
    packed, padded, column, gathered, table, channel, noise_f, out_f, out_v, row_send, rows, sum_send, sums,
    in_sems, send_sems, recv_sems, ready,
):
    n_freq, n_drop = lax.axis_size("freq"), lax.axis_size("drop")
    freq, drop = lax.axis_index("freq"), lax.axis_index("drop")
    barrier = pltpu.get_barrier_semaphore()

    x, y = freq // NY, lax.rem(freq, NY)

    def peer(dx, dy):
        return {"freq": lax.rem(x + dx, NX) * NY + lax.rem(y + dy, NY)}

    def signal(semaphore, device):
        pl.semaphore_signal(semaphore, inc=1, device_id=device, device_id_type=MESH)

    for dx, dy in ALONG_Y + ALONG_X:
        signal(barrier, peer(dx, dy))

    @pl.loop(drop + 1, n_drop)
    def _(i):
        signal(barrier, {"drop": i})

    loads = [
        pltpu.make_async_copy(src, dst, in_sems.at[i])
        for i, (src, dst) in enumerate(
            (
                (taps_hbm, taps_v), (lags_hbm, lags_v), (gain_hbm, gain_v),
                (symbols_hbm, symbols_v), (noise_hbm, noise_v), (std_hbm, std_v),
            )
        )
    ]
    for load in loads:
        load.start()

    padded[...] = jnp.zeros_like(padded)
    loads[0].wait()
    for q in range(4):
        padded[q, :, 0:TAPS] = taps_v[q // 2, q % 2]
    own = padded[0]
    for q in range(1, 4):
        own = own + pltpu.roll(padded[q], 32 * q, 1)
    packed[...] = own
    gathered[freq] = own

    pl.semaphore_wait(barrier, NX + NY - 2 + drop)

    def copy_to(device, src, dst, i):
        return pltpu.make_async_remote_copy(
            src_ref=src, dst_ref=dst, send_sem=send_sems.at[i], recv_sem=recv_sems.at[i],
            device_id=device, device_id_type=MESH,
        )

    def all_of(ref, n, i):
        return copy_to(peer(0, 1), ref.at[pl.ds(0, n)], ref.at[pl.ds(0, n)], i)

    for dx, dy in ALONG_Y:
        copy_to(peer(dx, dy), packed, gathered.at[freq], 0).start()

    @pl.loop(0, drop)
    def _(i):
        signal(ready, {"drop": i})

    loads[1].wait()
    loads[2].wait()
    loads[5].wait()
    column[...] = jnp.zeros_like(column)
    column[0:2, 0:TAPS] = lags_v[...].astype(F32)
    column[2:4, 0:SNRS] = std_v[...]
    turned = jnp.transpose(column[...])
    gain = gain_v[...]
    tone = freq * LANES + lax.broadcasted_iota(jnp.int32, (32, LANES), 1)
    table[...] = jnp.zeros_like(table)
    for d in range(2):
        lag = turned[0:32, d : d + 1].astype(jnp.int32)
        cosine, sine = cos_sin((lag * tone) & (FOURIER_POINTS - 1))
        cosine = cosine * gain
        sine = sine * gain
        table[64 * d : 64 * d + 32, 256 * d : 256 * d + 128] = cosine
        table[64 * d + 32 : 64 * d + 64, 256 * d : 256 * d + 128] = sine
        table[64 * d : 64 * d + 32, 256 * d + 128 : 256 * d + 256] = -sine
        table[64 * d + 32 : 64 * d + 64, 256 * d + 128 : 256 * d + 256] = cosine
    std = [jnp.broadcast_to(turned[0:SNRS, 2 + d : 3 + d], (SNRS, LANES)).reshape(2, 8, LANES) for d in range(2)]

    loads[4].wait()

    @pl.loop(0, 32)
    def _(i):
        at = pl.ds(pl.multiple_of(i * 64, 64), 64)
        noise_f[at, :] = noise_v[at, :].astype(F32)

    all_of(gathered, NY - 1, 0).wait_recv()
    mine = gathered.at[pl.ds(x * NY, NY)]
    for dx, dy in ALONG_X:
        copy_to(peer(dx, dy), mine, mine, 1).start()
    all_of(gathered, (NX - 1) * NY, 1).wait_recv()
    response = jnp.dot(
        gathered[...].reshape(RX * TX, LANES), table[...],
        precision=lax.Precision.HIGHEST, preferred_element_type=F32,
    )
    for q in range(4):
        channel[q] = response[:, LANES * q : LANES * (q + 1)]

    def match_step(r, so_far):
        result = []
        for d in range(2):
            noise = [noise_f[pl.ds(1024 * d + 32 * c + r, SNRS, stride=64), :].reshape(2, 8, LANES) for c in range(2)]
            for t in range(TX):
                h = [channel[2 * d + c, pl.ds(TX * r + t, 1), :] for c in range(2)]
                h = [jnp.broadcast_to(v, (8, LANES))[None] for v in h]
                re, im = cmul_conj(h, noise)
                old_re, old_im = so_far[4 * d + t]
                result.append((old_re + re, old_im + im))
        return tuple(result)

    nothing = jnp.zeros((2, 8, LANES), F32)
    match = lax.fori_loop(0, RX, match_step, ((nothing, nothing),) * 8, unroll=4)

    solved, totals, powers = [], [], []
    for d in range(2):
        h = [[channel[2 * d + c, pl.ds(t, RX, stride=TX), :] for c in range(2)] for t in range(TX)]
        diagonal = [over_sublanes(h[t][0] * h[t][0] + h[t][1] * h[t][1]) for t in range(TX)]
        upper = {}
        for t in range(TX):
            for u in range(t + 1, TX):
                re, im = cmul_conj(h[t], h[u])
                upper[t, u] = over_sublanes(re), over_sublanes(im)
        powers.append((diagonal[0] + diagonal[1]) + (diagonal[2] + diagonal[3]))
        right = [match[4 * d + t] for t in range(TX)]
        inverse = []
        for i in range(TX):
            inverse.append(1.0 / diagonal[i])
            for j in range(i + 1, TX):
                factor = upper[i, j][0] * inverse[i], -upper[i, j][1] * inverse[i]
                diagonal[j] = diagonal[j] - (factor[0] * upper[i, j][0] - factor[1] * upper[i, j][1])
                for k in range(j + 1, TX):
                    upper[j, k] = csub(upper[j, k], cmul(factor, upper[i, k]))
                right[j] = csub(right[j], cmul(factor, right[i]))
        result = [None] * TX
        for i in reversed(range(TX)):
            partial = right[i]
            for k in range(i + 1, TX):
                partial = csub(partial, cmul(upper[i, k], result[k]))
            result[i] = partial[0] * inverse[i], partial[1] * inverse[i]
        solved.append(result)
        total = result[0][0] * result[0][0] + result[0][1] * result[0][1]
        for t in range(1, TX):
            total = total + result[t][0] * result[t][0] + result[t][1] * result[t][1]
        totals.append(total * (std[d] * std[d]))

    lane8 = lax.broadcasted_iota(jnp.int32, (8, LANES), 1)
    sub8 = lax.broadcasted_iota(jnp.int32, (8, LANES), 0)
    power_rows = jnp.where(sub8 == 0, powers[0], jnp.where(sub8 == 1, powers[1], 0.0))
    stacked = [totals[0][0], totals[0][1], totals[1][0], totals[1][1], power_rows]
    row = jnp.zeros((8, LANES), F32)
    for i, piece in enumerate(stacked):
        row = row + jnp.where(lane8 == sub8 + 8 * i, jnp.sum(piece, axis=1, keepdims=True), 0.0)
    row = jnp.sum(row, axis=0, keepdims=True)
    row_send[...] = row
    rows[freq] = row

    @pl.loop(0, n_freq - 1)
    def _(i):
        far_x, far_y = lax.rem(i, NX), i // NX
        dx = NX // 2 + (far_x + 1) // 2 * (2 * lax.rem(far_x, 2) - 1)
        dy = NY // 2 + (far_y + 1) // 2 * (2 * lax.rem(far_y, 2) - 1)
        copy_to(peer(dx, dy), row_send, rows.at[freq], 2).start()

    loads[3].wait()
    sent = []
    for d in range(2):
        for t in range(TX):
            symbol = symbols_v[pl.ds(64 * d + t, SNRS, stride=TX), :]
            sent.append(
                (
                    (2 * (symbol & 3) - 3).astype(F32) * level_scale,
                    (2 * lax.shift_right_logical(symbol, 2) - 3).astype(F32) * level_scale,
                )
            )

    all_of(rows, n_freq - 1, 2).wait_recv()
    row = jnp.sum(rows[...], axis=0)
    lane = lax.broadcasted_iota(jnp.int32, (1, LANES), 1)
    power = [
        jnp.sum(jnp.where(lane == 32 + d, row, 0.0), axis=1, keepdims=True) * (1.0 / (FOURIER_POINTS * RX * TX))
        for d in range(2)
    ]
    weighted = row * jnp.where(lane < SNRS, power[0], jnp.where(lane < 2 * SNRS, power[1], 0.0))
    sum_send[...] = weighted
    sums[drop] = weighted

    @pl.loop(0, drop)
    def _(i):
        copy_to({"drop": i}, sum_send, sums.at[drop], 3).start()

    @pl.when(drop < n_drop - 1)
    def _():
        pl.semaphore_wait(ready, n_drop - 1 - drop)

    @pl.loop(drop + 1, n_drop)
    def _(i):
        copy_to({"drop": i}, sum_send, sums.at[drop], 3).start()

    for d in range(2):
        amplitude = std[d] * jnp.sqrt(jnp.broadcast_to(power[d], (8, LANES)))
        for t in range(TX):
            for c in range(2):
                estimate = sent[4 * d + t][c] + (amplitude * solved[d][t][c]).reshape(SNRS, LANES)
                out_f[pl.ds(128 * d + 4 * c + t, SNRS, stride=8), :] = estimate
    out_v[...] = out_f[...].astype(jnp.bfloat16)
    store = pltpu.make_async_copy(out_v, detected_ref, in_sems.at[6])
    store.start()

    all_of(sums, n_drop - 1, 3).wait_recv()
    total = jnp.sum(sums[...], axis=0)
    total = total[:, 0:SNRS] + total[:, SNRS : 2 * SNRS]
    error_ref[...] = RX * total / (DROPS * TX * FOURIER_POINTS)

    store.wait()
    all_of(gathered, NY - 1, 0).wait_send()
    all_of(gathered, (NX - 1) * NY, 1).wait_send()
    all_of(rows, n_freq - 1, 2).wait_send()
    all_of(sums, n_drop - 1, 3).wait_send()


def shards(taps, echo_lags, front_gain, symbols, noise, noise_std):
    n_freq, n_drop = lax.axis_size("freq"), lax.axis_size("drop")
    vmem = pltpu.VMEM
    detected, error = pl.pallas_call(
        kernel,
        out_shape=(
            jax.ShapeDtypeStruct((2 * SNRS * 8, LANES), jnp.bfloat16),
            jax.ShapeDtypeStruct((1, SNRS), F32),
        ),
        in_specs=[pl.BlockSpec(memory_space=pltpu.HBM)] * 6,
        out_specs=(pl.BlockSpec(memory_space=pl.ANY), pl.BlockSpec(memory_space=pltpu.VMEM)),
        scratch_shapes=[
            vmem((2, 2, TX, TAPS), F32),
            vmem((2, TAPS), jnp.int32),
            vmem((1, LANES), F32),
            vmem((2 * SNRS * TX, LANES), jnp.int32),
            vmem((2 * SNRS * 2 * RX, LANES), jnp.bfloat16),
            vmem((2, SNRS), F32),
            vmem((TX, LANES), F32),
            vmem((4, TX, LANES), F32),
            vmem((LANES, LANES), F32),
            vmem((n_freq, TX, LANES), F32),
            vmem((LANES, 4 * LANES), F32),
            vmem((4, RX * TX, LANES), F32),
            vmem((2 * SNRS * 2 * RX, LANES), F32),
            vmem((2 * SNRS * 8, LANES), F32),
            vmem((2 * SNRS * 8, LANES), jnp.bfloat16),
            vmem((1, LANES), F32),
            vmem((n_freq, 1, LANES), F32),
            vmem((1, LANES), F32),
            vmem((n_drop, 1, LANES), F32),
            pltpu.SemaphoreType.DMA((7,)),
            pltpu.SemaphoreType.DMA((4,)),
            pltpu.SemaphoreType.DMA((4,)),
            pltpu.SemaphoreType.REGULAR,
        ],
        compiler_params=pltpu.CompilerParams(collective_id=0, has_side_effects=True, vmem_limit_bytes=16 << 20),
    )(
        *[
            pltpu.with_memory_space_constraint(v, pltpu.HBM)
            for v in (
                jnp.transpose(taps, (0, 1, 3, 2)),
                echo_lags,
                front_gain.reshape(1, LANES),
                symbols.reshape(2 * SNRS * TX, LANES),
                noise.reshape(2 * SNRS * 2 * RX, LANES),
                noise_std,
            )
        ]
    )
    return detected.reshape(2, SNRS, 2, TX, LANES), error.reshape(SNRS)


def solution(mesh):
    placed = (
        P("drop", None, None, "freq"),
        P("drop", None),
        P("freq"),
        P("drop", None, None, "freq"),
        P("drop", None, None, None, "freq"),
        P("drop", None),
    )
    return jax.shard_map(
        shards,
        mesh=mesh,
        in_specs=placed,
        out_specs=(P("drop", None, None, None, "freq"), P()),
        check_vma=False,
    )
```

```python
import math

import jax
import jax.numpy as jnp
from jax import lax
from jax.experimental import pallas as pl
from jax.experimental.pallas import tpu as pltpu
from jax.sharding import PartitionSpec as P

RX = 32
TX = 4
TAPS = 23
SNRS = 16
FOURIER_POINTS = 4096
DROPS = 32
LANES = 128
NX, NY = 4, 8
ALONG_X = ((2, 0), (1, 0), (3, 0))
MESH = pl.DeviceIdType.MESH
F32 = jnp.float32

level_scale = 1.0 / math.sqrt(10.0)


def cos_sin(cycles):
    shifted = cycles + 512
    quadrant = lax.shift_right_logical(shifted, 10) & 3
    x = ((shifted & 1023) - 512).astype(F32) * (2.0 * math.pi / FOURIER_POINTS)
    x2 = x * x
    s = x * (1.0 + x2 * (-1 / 6 + x2 * (1 / 120 + x2 * (-1 / 5040 + x2 * (1 / 362880)))))
    c = 1.0 + x2 * (-0.5 + x2 * (1 / 24 + x2 * (-1 / 720 + x2 * (1 / 40320 + x2 * (-1 / 3628800)))))
    odd = (quadrant & 1) == 1
    cosine = jnp.where(odd, s, c)
    sine = jnp.where(odd, c, s)
    cosine = jnp.where((quadrant == 1) | (quadrant == 2), -cosine, cosine)
    sine = jnp.where(quadrant >= 2, -sine, sine)
    return cosine, sine


def over_sublanes(x):
    x = (x[0:8] + x[8:16]) + (x[16:24] + x[24:32])
    x = x + pltpu.roll(x, 4, 0)
    x = x + pltpu.roll(x, 2, 0)
    return x + pltpu.roll(x, 1, 0)


def cmul(a, b):
    return a[0] * b[0] - a[1] * b[1], a[0] * b[1] + a[1] * b[0]


def cmul_conj(a, b):
    return a[0] * b[0] + a[1] * b[1], a[0] * b[1] - a[1] * b[0]


def csub(a, b):
    return a[0] - b[0], a[1] - b[1]


def kernel(
    taps_hbm, lags_hbm, gain_hbm, symbols_hbm, noise_hbm, std_hbm,
    detected_ref, error_ref,
    taps_v, lags_v, gain_v, symbols_v, noise_v, std_v,
    packed, padded, column, gathered, table, channel, noise_f, out_f, out_v, row_send, rows, sum_send, sums,
    in_sems, send_sems, recv_sems, y_ready, ready,
):
    n_freq, n_drop = lax.axis_size("freq"), lax.axis_size("drop")
    freq, drop = lax.axis_index("freq"), lax.axis_index("drop")
    barrier = pltpu.get_barrier_semaphore()

    x, y = freq // NY, lax.rem(freq, NY)

    def peer(dx, dy):
        return {"freq": lax.rem(x + dx, NX) * NY + lax.rem(y + dy, NY)}

    def signal(semaphore, device):
        pl.semaphore_signal(semaphore, inc=1, device_id=device, device_id_type=MESH)

    loads = [
        pltpu.make_async_copy(src, dst, in_sems.at[i])
        for i, (src, dst) in enumerate(
            (
                (taps_hbm, taps_v), (lags_hbm, lags_v), (gain_hbm, gain_v),
                (symbols_hbm, symbols_v), (noise_hbm, noise_v), (std_hbm, std_v),
            )
        )
    ]
    for load in loads:
        load.start()

    upper = y // 5
    order = (1 - upper) * (2 * y - 1 + (NY - y) // NY) + upper * 2 * (NY - y)

    def y_peer(i):
        odd = lax.rem(i, 2)
        return {"freq": x * NY + odd * ((i + 1) // 2) + (1 - odd) * lax.rem(NY - i // 2, NY)}

    for dx, dy in ALONG_X:
        signal(barrier, peer(dx, dy))

    @pl.loop(order + 1, NY)
    def _(i):
        signal(barrier, y_peer(i))

    @pl.loop(drop + 1, n_drop)
    def _(i):
        signal(barrier, {"drop": i})

    padded[...] = jnp.zeros_like(padded)
    loads[0].wait()
    for q in range(4):
        padded[q, :, 0:TAPS] = taps_v[q // 2, q % 2]
    own = padded[0]
    for q in range(1, 4):
        own = own + pltpu.roll(padded[q], 32 * q, 1)
    packed[...] = own
    gathered[y, x] = own

    pl.semaphore_wait(barrier, NX - 1 + order + drop)

    def copy_to(device, src, dst, i):
        return pltpu.make_async_remote_copy(
            src_ref=src, dst_ref=dst, send_sem=send_sems.at[i], recv_sem=recv_sems.at[i],
            device_id=device, device_id_type=MESH,
        )

    def all_of(ref, n, i):
        return copy_to(peer(0, 1), ref.at[pl.ds(0, n)], ref.at[pl.ds(0, n)], i)

    for dx, dy in ALONG_X:
        copy_to(peer(dx, dy), packed, gathered.at[y, x], 0).start()

    @pl.loop(0, order)
    def _(i):
        signal(y_ready, y_peer(i))

    @pl.loop(0, drop)
    def _(i):
        signal(ready, {"drop": i})

    loads[1].wait()
    loads[2].wait()
    loads[5].wait()
    column[...] = jnp.zeros_like(column)
    column[0:2, 0:TAPS] = lags_v[...].astype(F32)
    column[2:4, 0:SNRS] = std_v[...]
    turned = jnp.transpose(column[...])
    gain = gain_v[...]
    tone = freq * LANES + lax.broadcasted_iota(jnp.int32, (32, LANES), 1)
    table[...] = jnp.zeros_like(table)
    for d in range(2):
        lag = turned[0:32, d : d + 1].astype(jnp.int32)
        cosine, sine = cos_sin((lag * tone) & (FOURIER_POINTS - 1))
        cosine = cosine * gain
        sine = sine * gain
        table[64 * d : 64 * d + 32, 256 * d : 256 * d + 128] = cosine
        table[64 * d + 32 : 64 * d + 64, 256 * d : 256 * d + 128] = sine
        table[64 * d : 64 * d + 32, 256 * d + 128 : 256 * d + 256] = -sine
        table[64 * d + 32 : 64 * d + 64, 256 * d + 128 : 256 * d + 256] = cosine
    std = [jnp.broadcast_to(turned[0:SNRS, 2 + d : 3 + d], (SNRS, LANES)).reshape(2, 8, LANES) for d in range(2)]

    loads[4].wait()

    @pl.loop(0, 32)
    def _(i):
        at = pl.ds(pl.multiple_of(i * 64, 64), 64)
        noise_f[at, :] = noise_v[at, :].astype(F32)

    all_of(gathered.at[0], NX - 1, 0).wait_recv()

    @pl.loop(0, order)
    def _(i):
        copy_to(y_peer(i), gathered.at[y], gathered.at[y], 1).start()

    @pl.when(order < NY - 1)
    def _():
        pl.semaphore_wait(y_ready, NY - 1 - order)

    @pl.loop(0, NY - 1 - order)
    def _(i):
        copy_to(y_peer(NY - 1 - i), gathered.at[y], gathered.at[y], 1).start()

    all_of(gathered, NY - 1, 1).wait_recv()
    response = jnp.dot(
        gathered[...].reshape(RX * TX, LANES), table[...],
        precision=lax.Precision.HIGHEST, preferred_element_type=F32,
    )
    for q in range(4):
        channel[q] = response[:, LANES * q : LANES * (q + 1)]

    def match_step(i, so_far):
        r = lax.rem(i, NX) * NY + i // NX
        result = []
        for d in range(2):
            noise = [noise_f[pl.ds(1024 * d + 32 * c + r, SNRS, stride=64), :].reshape(2, 8, LANES) for c in range(2)]
            for t in range(TX):
                h = [channel[2 * d + c, pl.ds(TX * i + t, 1), :] for c in range(2)]
                h = [jnp.broadcast_to(v, (8, LANES))[None] for v in h]
                re, im = cmul_conj(h, noise)
                old_re, old_im = so_far[4 * d + t]
                result.append((old_re + re, old_im + im))
        return tuple(result)

    nothing = jnp.zeros((2, 8, LANES), F32)
    match = lax.fori_loop(0, RX, match_step, ((nothing, nothing),) * 8, unroll=4)

    solved, totals, powers = [], [], []
    for d in range(2):
        h = [[channel[2 * d + c, pl.ds(t, RX, stride=TX), :] for c in range(2)] for t in range(TX)]
        diagonal = [over_sublanes(h[t][0] * h[t][0] + h[t][1] * h[t][1]) for t in range(TX)]
        upper = {}
        for t in range(TX):
            for u in range(t + 1, TX):
                re, im = cmul_conj(h[t], h[u])
                upper[t, u] = over_sublanes(re), over_sublanes(im)
        powers.append((diagonal[0] + diagonal[1]) + (diagonal[2] + diagonal[3]))
        right = [match[4 * d + t] for t in range(TX)]
        inverse = []
        for i in range(TX):
            inverse.append(1.0 / diagonal[i])
            for j in range(i + 1, TX):
                factor = upper[i, j][0] * inverse[i], -upper[i, j][1] * inverse[i]
                diagonal[j] = diagonal[j] - (factor[0] * upper[i, j][0] - factor[1] * upper[i, j][1])
                for k in range(j + 1, TX):
                    upper[j, k] = csub(upper[j, k], cmul(factor, upper[i, k]))
                right[j] = csub(right[j], cmul(factor, right[i]))
        result = [None] * TX
        for i in reversed(range(TX)):
            partial = right[i]
            for k in range(i + 1, TX):
                partial = csub(partial, cmul(upper[i, k], result[k]))
            result[i] = partial[0] * inverse[i], partial[1] * inverse[i]
        solved.append(result)
        total = result[0][0] * result[0][0] + result[0][1] * result[0][1]
        for t in range(1, TX):
            total = total + result[t][0] * result[t][0] + result[t][1] * result[t][1]
        totals.append(total * (std[d] * std[d]))

    lane8 = lax.broadcasted_iota(jnp.int32, (8, LANES), 1)
    sub8 = lax.broadcasted_iota(jnp.int32, (8, LANES), 0)
    power_rows = jnp.where(sub8 == 0, powers[0], jnp.where(sub8 == 1, powers[1], 0.0))
    stacked = [totals[0][0], totals[0][1], totals[1][0], totals[1][1], power_rows]
    row = jnp.zeros((8, LANES), F32)
    for i, piece in enumerate(stacked):
        row = row + jnp.where(lane8 == sub8 + 8 * i, jnp.sum(piece, axis=1, keepdims=True), 0.0)
    row = jnp.sum(row, axis=0, keepdims=True)
    row_send[...] = row
    rows[freq] = row

    @pl.loop(0, n_freq - 1)
    def _(i):
        far_x, far_y = lax.rem(i, NX), i // NX
        dx = NX // 2 + (far_x + 1) // 2 * (2 * lax.rem(far_x, 2) - 1)
        dy = NY // 2 + (far_y + 1) // 2 * (2 * lax.rem(far_y, 2) - 1)
        copy_to(peer(dx, dy), row_send, rows.at[freq], 2).start()

    loads[3].wait()
    sent = []
    for d in range(2):
        for t in range(TX):
            symbol = symbols_v[pl.ds(64 * d + t, SNRS, stride=TX), :]
            sent.append(
                (
                    (2 * (symbol & 3) - 3).astype(F32) * level_scale,
                    (2 * lax.shift_right_logical(symbol, 2) - 3).astype(F32) * level_scale,
                )
            )

    all_of(rows, n_freq - 1, 2).wait_recv()
    row = jnp.sum(rows[...], axis=0)
    lane = lax.broadcasted_iota(jnp.int32, (1, LANES), 1)
    power = [
        jnp.sum(jnp.where(lane == 32 + d, row, 0.0), axis=1, keepdims=True) * (1.0 / (FOURIER_POINTS * RX * TX))
        for d in range(2)
    ]
    weighted = row * jnp.where(lane < SNRS, power[0], jnp.where(lane < 2 * SNRS, power[1], 0.0))
    sum_send[...] = weighted
    sums[drop] = weighted

    @pl.loop(0, drop)
    def _(i):
        copy_to({"drop": i}, sum_send, sums.at[drop], 3).start()

    @pl.when(drop < n_drop - 1)
    def _():
        pl.semaphore_wait(ready, n_drop - 1 - drop)

    @pl.loop(drop + 1, n_drop)
    def _(i):
        copy_to({"drop": i}, sum_send, sums.at[drop], 3).start()

    for d in range(2):
        amplitude = std[d] * jnp.sqrt(jnp.broadcast_to(power[d], (8, LANES)))
        for t in range(TX):
            for c in range(2):
                estimate = sent[4 * d + t][c] + (amplitude * solved[d][t][c]).reshape(SNRS, LANES)
                out_f[pl.ds(128 * d + 4 * c + t, SNRS, stride=8), :] = estimate
    out_v[...] = out_f[...].astype(jnp.bfloat16)
    store = pltpu.make_async_copy(out_v, detected_ref, in_sems.at[6])
    store.start()

    all_of(sums, n_drop - 1, 3).wait_recv()
    total = jnp.sum(sums[...], axis=0)
    total = total[:, 0:SNRS] + total[:, SNRS : 2 * SNRS]
    error_ref[...] = RX * total / (DROPS * TX * FOURIER_POINTS)

    store.wait()
    all_of(gathered.at[0], NX - 1, 0).wait_send()
    all_of(gathered, NY - 1, 1).wait_send()
    all_of(rows, n_freq - 1, 2).wait_send()
    all_of(sums, n_drop - 1, 3).wait_send()


def shards(taps, echo_lags, front_gain, symbols, noise, noise_std):
    n_freq, n_drop = lax.axis_size("freq"), lax.axis_size("drop")
    vmem = pltpu.VMEM
    detected, error = pl.pallas_call(
        kernel,
        out_shape=(
            jax.ShapeDtypeStruct((2 * SNRS * 8, LANES), jnp.bfloat16),
            jax.ShapeDtypeStruct((1, SNRS), F32),
        ),
        in_specs=[pl.BlockSpec(memory_space=pltpu.HBM)] * 6,
        out_specs=(pl.BlockSpec(memory_space=pl.ANY), pl.BlockSpec(memory_space=pltpu.VMEM)),
        scratch_shapes=[
            vmem((2, 2, TX, TAPS), F32),
            vmem((2, TAPS), jnp.int32),
            vmem((1, LANES), F32),
            vmem((2 * SNRS * TX, LANES), jnp.int32),
            vmem((2 * SNRS * 2 * RX, LANES), jnp.bfloat16),
            vmem((2, SNRS), F32),
            vmem((TX, LANES), F32),
            vmem((4, TX, LANES), F32),
            vmem((LANES, LANES), F32),
            vmem((NY, NX, TX, LANES), F32),
            vmem((LANES, 4 * LANES), F32),
            vmem((4, RX * TX, LANES), F32),
            vmem((2 * SNRS * 2 * RX, LANES), F32),
            vmem((2 * SNRS * 8, LANES), F32),
            vmem((2 * SNRS * 8, LANES), jnp.bfloat16),
            vmem((1, LANES), F32),
            vmem((n_freq, 1, LANES), F32),
            vmem((1, LANES), F32),
            vmem((n_drop, 1, LANES), F32),
            pltpu.SemaphoreType.DMA((7,)),
            pltpu.SemaphoreType.DMA((4,)),
            pltpu.SemaphoreType.DMA((4,)),
            pltpu.SemaphoreType.REGULAR,
            pltpu.SemaphoreType.REGULAR,
        ],
        compiler_params=pltpu.CompilerParams(collective_id=0, has_side_effects=True, vmem_limit_bytes=16 << 20),
    )(
        *[
            pltpu.with_memory_space_constraint(v, pltpu.HBM)
            for v in (
                jnp.transpose(taps, (0, 1, 3, 2)),
                echo_lags,
                front_gain.reshape(1, LANES),
                symbols.reshape(2 * SNRS * TX, LANES),
                noise.reshape(2 * SNRS * 2 * RX, LANES),
                noise_std,
            )
        ]
    )
    return detected.reshape(2, SNRS, 2, TX, LANES), error.reshape(SNRS)


def solution(mesh):
    placed = (
        P("drop", None, None, "freq"),
        P("drop", None),
        P("freq"),
        P("drop", None, None, "freq"),
        P("drop", None, None, None, "freq"),
        P("drop", None),
    )
    return jax.shard_map(
        shards,
        mesh=mesh,
        in_specs=placed,
        out_specs=(P("drop", None, None, None, "freq"), P()),
        check_vma=False,
    )
```

```python
import math

import jax
import jax.numpy as jnp
from jax import lax
from jax.experimental import pallas as pl
from jax.experimental.pallas import tpu as pltpu
from jax.sharding import PartitionSpec as P

RX = 32
TX = 4
TAPS = 23
SNRS = 16
FOURIER_POINTS = 4096
DROPS = 32
LANES = 128
NX, NY = 4, 8
NEAR = 6
ALONG_X = ((2, 0), (1, 0), (3, 0))
MESH = pl.DeviceIdType.MESH
F32 = jnp.float32

level_scale = 1.0 / math.sqrt(10.0)


def cos_sin(cycles):
    shifted = cycles + 512
    quadrant = lax.shift_right_logical(shifted, 10) & 3
    x = ((shifted & 1023) - 512).astype(F32) * (2.0 * math.pi / FOURIER_POINTS)
    x2 = x * x
    s = x * (1.0 + x2 * (-1 / 6 + x2 * (1 / 120 + x2 * (-1 / 5040 + x2 * (1 / 362880)))))
    c = 1.0 + x2 * (-0.5 + x2 * (1 / 24 + x2 * (-1 / 720 + x2 * (1 / 40320 + x2 * (-1 / 3628800)))))
    odd = (quadrant & 1) == 1
    cosine = jnp.where(odd, s, c)
    sine = jnp.where(odd, c, s)
    cosine = jnp.where((quadrant == 1) | (quadrant == 2), -cosine, cosine)
    sine = jnp.where(quadrant >= 2, -sine, sine)
    return cosine, sine


def over_sublanes(x):
    x = x + pltpu.roll(x, 4, 0)
    x = x + pltpu.roll(x, 2, 0)
    return x + pltpu.roll(x, 1, 0)


def cmul(a, b):
    return a[0] * b[0] - a[1] * b[1], a[0] * b[1] + a[1] * b[0]


def cmul_conj(a, b):
    return a[0] * b[0] + a[1] * b[1], a[0] * b[1] - a[1] * b[0]


def cadd(a, b):
    return a[0] + b[0], a[1] + b[1]


def halves(x):
    high = x.astype(jnp.bfloat16)
    return high, (x - high.astype(F32)).astype(jnp.bfloat16)


def csub(a, b):
    return a[0] - b[0], a[1] - b[1]


def kernel(
    taps_hbm, lags_hbm, gain_hbm, symbols_hbm, noise_hbm, std_hbm,
    detected_ref, error_ref,
    taps_v, lags_v, gain_v, symbols_v, noise_v, std_v,
    packed, padded, column, gathered, table, channel, noise_f, out_f, out_v, row_send, rows, sum_send, sums,
    in_sems, send_sems, recv_sems, y_ready, ready,
):
    n_freq, n_drop = lax.axis_size("freq"), lax.axis_size("drop")
    freq, drop = lax.axis_index("freq"), lax.axis_index("drop")
    barrier = pltpu.get_barrier_semaphore()

    x, y = freq // NY, lax.rem(freq, NY)

    def peer(dx, dy):
        return {"freq": lax.rem(x + dx, NX) * NY + lax.rem(y + dy, NY)}

    def signal(semaphore, device):
        pl.semaphore_signal(semaphore, inc=1, device_id=device, device_id_type=MESH)

    loads = [
        pltpu.make_async_copy(src, dst, in_sems.at[i])
        for i, (src, dst) in enumerate(
            (
                (taps_hbm, taps_v), (lags_hbm, lags_v), (gain_hbm, gain_v),
                (symbols_hbm, symbols_v), (noise_hbm, noise_v), (std_hbm, std_v),
            )
        )
    ]
    for load in loads:
        load.start()

    upper = y // 5
    order = (1 - upper) * (2 * y - 1 + (NY - y) // NY) + upper * 2 * (NY - y)

    def y_at(i):
        odd = lax.rem(i, 2)
        return odd * ((i + 1) // 2) + (1 - odd) * lax.rem(NY - i // 2, NY)

    def y_peer(i):
        return {"freq": x * NY + y_at(i)}

    for dx, dy in ALONG_X:
        signal(barrier, peer(dx, dy))

    @pl.loop(order + 1, NY)
    def _(i):
        signal(barrier, y_peer(i))

    @pl.loop(drop + 1, n_drop)
    def _(i):
        signal(barrier, {"drop": i})

    padded[...] = jnp.zeros_like(padded)
    loads[0].wait()
    for q in range(4):
        padded[q, :, 0:TAPS] = taps_v[q // 2, q % 2]
    own = padded[0]
    for q in range(1, 4):
        own = own + pltpu.roll(padded[q], 32 * q, 1)
    packed[...] = own
    gathered[y, x] = own

    pl.semaphore_wait(barrier, NX - 1 + order + drop)

    def copy_to(device, src, dst, i, received=None):
        return pltpu.make_async_remote_copy(
            src_ref=src, dst_ref=dst, send_sem=send_sems.at[i], recv_sem=recv_sems.at[i if received is None else received],
            device_id=device, device_id_type=MESH,
        )

    def all_of(ref, n, i, received=None):
        return copy_to(peer(0, 1), ref.at[pl.ds(0, n)], ref.at[pl.ds(0, n)], i, received)

    for dx, dy in ALONG_X:
        copy_to(peer(dx, dy), packed, gathered.at[y, x], 0).start()

    @pl.loop(0, order)
    def _(i):
        signal(y_ready.at[order], y_peer(i))

    @pl.loop(0, drop)
    def _(i):
        signal(ready, {"drop": i})

    loads[1].wait()
    loads[2].wait()
    loads[5].wait()
    column[...] = jnp.zeros_like(column)
    column[0:2, 0:TAPS] = lags_v[...].astype(F32)
    column[2:4, 0:SNRS] = std_v[...]
    turned = jnp.transpose(column[...])
    gain = gain_v[...]
    tone = freq * LANES + lax.broadcasted_iota(jnp.int32, (32, LANES), 1)
    table[...] = jnp.zeros_like(table)
    for d in range(2):
        lag = turned[0:32, d : d + 1].astype(jnp.int32)
        cosine, sine = cos_sin((lag * tone) & (FOURIER_POINTS - 1))
        cosine = cosine * gain
        sine = sine * gain
        for at, block in ((0, (cosine, -sine)), (32, (sine, cosine))):
            for c in range(2):
                high, low = halves(block[c])
                lanes = slice(LANES * c, LANES * (c + 1))
                table[d, at : at + 32, lanes] = high
                table[d, at + 64 : at + 96, lanes] = high
                table[d, at + 128 + 64 * d : at + 160 + 64 * d, lanes] = low
    std = [jnp.broadcast_to(turned[0:SNRS, 2 + d : 3 + d], (SNRS, LANES)).reshape(2, 8, LANES) for d in range(2)]

    loads[4].wait()

    @pl.loop(0, 32)
    def _(i):
        at = pl.ds(pl.multiple_of(i * 64, 64), 64)
        noise_f[at, :] = noise_v[at, :].astype(F32)

    all_of(gathered.at[0], NX - 1, 0).wait_recv()

    def send_row_of_taps(i):
        late = lax.rem(y - y_at(i) + NY + 2, NY) // NEAR
        copy_to(y_peer(i), gathered.at[y], gathered.at[y], 1, 1 + 3 * late).start()

    @pl.loop(0, order)
    def _(i):
        send_row_of_taps(i)

    @pl.loop(order + 1, NY)
    def _(i):
        pl.semaphore_wait(y_ready.at[i], 1)
        send_row_of_taps(i)

    def respond(places):
        rows_of = [gathered[lax.rem(y + 6 + i, NY)].reshape(NX * TX, LANES) for i in places]
        full = jnp.concatenate(rows_of, axis=0)
        high = full.astype(jnp.bfloat16).astype(F32)
        low = pltpu.roll(full - high, 64, 1)
        first = lax.broadcasted_iota(jnp.int32, full.shape, 1) < 64
        at = slice(NX * TX * places[0], NX * TX * (places[-1] + 1))
        for d in range(2):
            mixed = jnp.where(first, high, low) if d == 0 else jnp.where(first, low, high)
            left = jnp.concatenate([mixed, high], axis=1).astype(jnp.bfloat16)
            response = jnp.dot(left, table[d], preferred_element_type=F32)
            for c in range(2):
                channel[2 * d + c, at, :] = response[:, LANES * c : LANES * (c + 1)]

    def gram_terms(groups):
        result = []
        for d in range(2):
            diagonal, upper = [0.0] * TX, {}
            for g in groups:
                h = [[channel[2 * d + c, pl.ds(32 * g + t, 8, stride=TX), :] for c in range(2)] for t in range(TX)]
                for t in range(TX):
                    diagonal[t] = diagonal[t] + h[t][0] * h[t][0] + h[t][1] * h[t][1]
                    for u in range(t + 1, TX):
                        upper[t, u] = cadd(upper.get((t, u), (0.0, 0.0)), cmul_conj(h[t], h[u]))
            result.append((diagonal, upper))
        return result
    def match_step(i, so_far):
        r = lax.rem(i, NX) * NY + lax.rem(y + 6 + i // NX, NY)
        result = []
        for d in range(2):
            noise = [noise_f[pl.ds(1024 * d + 32 * c + r, SNRS, stride=64), :].reshape(2, 8, LANES) for c in range(2)]
            for t in range(TX):
                h = [channel[2 * d + c, pl.ds(TX * i + t, 1), :] for c in range(2)]
                h = [jnp.broadcast_to(v, (8, LANES))[None] for v in h]
                re, im = cmul_conj(h, noise)
                old_re, old_im = so_far[4 * d + t]
                result.append((old_re + re, old_im + im))
        return tuple(result)

    nothing = jnp.zeros((2, 8, LANES), F32)
    all_of(gathered, NEAR - 1, 1).wait_recv()
    respond(range(NEAR))
    early = gram_terms(range(NEAR // 2))
    match = lax.fori_loop(0, NX * NEAR, match_step, ((nothing, nothing),) * 8, unroll=4)

    all_of(gathered, NY - NEAR, 1, 4).wait_recv()
    respond(range(NEAR, NY))
    late = gram_terms(range(NEAR // 2, NY // 2))
    match = lax.fori_loop(NX * NEAR, RX, match_step, match, unroll=True)

    solved, totals, powers = [], [], []
    for d in range(2):
        diagonal = [over_sublanes(early[d][0][t] + late[d][0][t]) for t in range(TX)]
        upper = {at: tuple(over_sublanes(v) for v in cadd(early[d][1][at], late[d][1][at])) for at in early[d][1]}
        powers.append((diagonal[0] + diagonal[1]) + (diagonal[2] + diagonal[3]))
        right = [match[4 * d + t] for t in range(TX)]
        inverse = []
        for i in range(TX):
            inverse.append(1.0 / diagonal[i])
            for j in range(i + 1, TX):
                factor = upper[i, j][0] * inverse[i], -upper[i, j][1] * inverse[i]
                diagonal[j] = diagonal[j] - (factor[0] * upper[i, j][0] - factor[1] * upper[i, j][1])
                for k in range(j + 1, TX):
                    upper[j, k] = csub(upper[j, k], cmul(factor, upper[i, k]))
                right[j] = csub(right[j], cmul(factor, right[i]))
        result = [None] * TX
        for i in reversed(range(TX)):
            partial = right[i]
            for k in range(i + 1, TX):
                partial = csub(partial, cmul(upper[i, k], result[k]))
            result[i] = partial[0] * inverse[i], partial[1] * inverse[i]
        solved.append(result)
        total = result[0][0] * result[0][0] + result[0][1] * result[0][1]
        for t in range(1, TX):
            total = total + result[t][0] * result[t][0] + result[t][1] * result[t][1]
        totals.append(total * (std[d] * std[d]))

    lane8 = lax.broadcasted_iota(jnp.int32, (8, LANES), 1)
    sub8 = lax.broadcasted_iota(jnp.int32, (8, LANES), 0)
    power_rows = jnp.where(sub8 == 0, powers[0], jnp.where(sub8 == 1, powers[1], 0.0))
    stacked = [totals[0][0], totals[0][1], totals[1][0], totals[1][1], power_rows]
    row = jnp.zeros((8, LANES), F32)
    for i, piece in enumerate(stacked):
        row = row + jnp.where(lane8 == sub8 + 8 * i, jnp.sum(piece, axis=1, keepdims=True), 0.0)
    row = jnp.sum(row, axis=0, keepdims=True)
    row_send[...] = row
    rows[freq] = row

    @pl.loop(0, n_freq - 1)
    def _(i):
        far_x, far_y = lax.rem(i, NX), i // NX
        dx = NX // 2 + (far_x + 1) // 2 * (2 * lax.rem(far_x, 2) - 1)
        dy = NY // 2 + (far_y + 1) // 2 * (2 * lax.rem(far_y, 2) - 1)
        copy_to(peer(dx, dy), row_send, rows.at[freq], 2).start()

    loads[3].wait()
    sent = []
    for d in range(2):
        for t in range(TX):
            symbol = symbols_v[pl.ds(64 * d + t, SNRS, stride=TX), :]
            sent.append(
                (
                    (2 * (symbol & 3) - 3).astype(F32) * level_scale,
                    (2 * lax.shift_right_logical(symbol, 2) - 3).astype(F32) * level_scale,
                )
            )

    all_of(rows, n_freq - 1, 2).wait_recv()
    row = jnp.sum(rows[...], axis=0)
    lane = lax.broadcasted_iota(jnp.int32, (1, LANES), 1)
    power = [
        jnp.sum(jnp.where(lane == 32 + d, row, 0.0), axis=1, keepdims=True) * (1.0 / (FOURIER_POINTS * RX * TX))
        for d in range(2)
    ]
    weighted = row * jnp.where(lane < SNRS, power[0], jnp.where(lane < 2 * SNRS, power[1], 0.0))
    sum_send[...] = weighted
    sums[drop] = weighted

    @pl.loop(0, drop)
    def _(i):
        copy_to({"drop": i}, sum_send, sums.at[drop], 3).start()

    @pl.when(drop < n_drop - 1)
    def _():
        pl.semaphore_wait(ready, n_drop - 1 - drop)

    @pl.loop(drop + 1, n_drop)
    def _(i):
        copy_to({"drop": i}, sum_send, sums.at[drop], 3).start()

    for d in range(2):
        amplitude = std[d] * jnp.sqrt(jnp.broadcast_to(power[d], (8, LANES)))
        for t in range(TX):
            for c in range(2):
                estimate = sent[4 * d + t][c] + (amplitude * solved[d][t][c]).reshape(SNRS, LANES)
                out_f[pl.ds(128 * d + 4 * c + t, SNRS, stride=8), :] = estimate
    out_v[...] = out_f[...].astype(jnp.bfloat16)
    store = pltpu.make_async_copy(out_v, detected_ref, in_sems.at[6])
    store.start()

    all_of(sums, n_drop - 1, 3).wait_recv()
    total = jnp.sum(sums[...], axis=0)
    total = total[:, 0:SNRS] + total[:, SNRS : 2 * SNRS]
    error_ref[...] = RX * total / (DROPS * TX * FOURIER_POINTS)

    store.wait()
    all_of(gathered.at[0], NX - 1, 0).wait_send()
    all_of(gathered, NY - 1, 1).wait_send()
    all_of(rows, n_freq - 1, 2).wait_send()
    all_of(sums, n_drop - 1, 3).wait_send()


def write_out(detected_ref, error_ref, detected_out, error_out, sems):
    copies = [
        pltpu.make_async_copy(src, dst, sems.at[i])
        for i, (src, dst) in enumerate(((detected_ref, detected_out), (error_ref, error_out)))
    ]
    for copy in copies:
        copy.start()
    for copy in copies:
        copy.wait()


def shards(taps, echo_lags, front_gain, symbols, noise, noise_std):
    n_freq, n_drop = lax.axis_size("freq"), lax.axis_size("drop")
    vmem = pltpu.VMEM
    detected, error = pl.pallas_call(
        kernel,
        out_shape=(
            jax.ShapeDtypeStruct((2 * SNRS * 8, LANES), jnp.bfloat16),
            jax.ShapeDtypeStruct((1, SNRS), F32),
        ),
        in_specs=[pl.BlockSpec(memory_space=pltpu.HBM)] * 6,
        out_specs=(pl.BlockSpec(memory_space=pl.ANY), pl.BlockSpec(memory_space=pltpu.VMEM)),
        scratch_shapes=[
            vmem((2, 2, TX, TAPS), F32),
            vmem((2, TAPS), jnp.int32),
            vmem((1, LANES), F32),
            vmem((2 * SNRS * TX, LANES), jnp.int32),
            vmem((2 * SNRS * 2 * RX, LANES), jnp.bfloat16),
            vmem((2, SNRS), F32),
            vmem((TX, LANES), F32),
            vmem((4, TX, LANES), F32),
            vmem((LANES, LANES), F32),
            vmem((NY, NX, TX, LANES), F32),
            vmem((2, 2 * LANES, 2 * LANES), jnp.bfloat16),
            vmem((4, RX * TX, LANES), F32),
            vmem((2 * SNRS * 2 * RX, LANES), F32),
            vmem((2 * SNRS * 8, LANES), F32),
            vmem((2 * SNRS * 8, LANES), jnp.bfloat16),
            vmem((1, LANES), F32),
            vmem((n_freq, 1, LANES), F32),
            vmem((1, LANES), F32),
            vmem((n_drop, 1, LANES), F32),
            pltpu.SemaphoreType.DMA((7,)),
            pltpu.SemaphoreType.DMA((4,)),
            pltpu.SemaphoreType.DMA((5,)),
            pltpu.SemaphoreType.REGULAR((NY,)),
            pltpu.SemaphoreType.REGULAR,
        ],
        compiler_params=pltpu.CompilerParams(collective_id=0, has_side_effects=True, vmem_limit_bytes=16 << 20),
    )(
        *[
            pltpu.with_memory_space_constraint(v, pltpu.HBM)
            for v in (
                jnp.transpose(taps, (0, 1, 3, 2)),
                echo_lags,
                front_gain.reshape(1, LANES),
                symbols.reshape(2 * SNRS * TX, LANES),
                noise.reshape(2 * SNRS * 2 * RX, LANES),
                noise_std,
            )
        ]
    )
    detected, error = pl.pallas_call(
        write_out,
        out_shape=(
            jax.ShapeDtypeStruct((2 * SNRS * 8, LANES), jnp.bfloat16),
            jax.ShapeDtypeStruct((1, SNRS), F32),
        ),
        in_specs=[pl.BlockSpec(memory_space=pltpu.VMEM)] * 2,
        out_specs=[pl.BlockSpec(memory_space=pltpu.HBM)] * 2,
        scratch_shapes=[pltpu.SemaphoreType.DMA((2,))],
        compiler_params=pltpu.CompilerParams(vmem_limit_bytes=1 << 20),
    )(detected, error)
    return detected.reshape(2, SNRS, 2, TX, LANES), error.reshape(SNRS)


def solution(mesh):
    placed = (
        P("drop", None, None, "freq"),
        P("drop", None),
        P("freq"),
        P("drop", None, None, "freq"),
        P("drop", None, None, None, "freq"),
        P("drop", None),
    )
    return jax.shard_map(
        shards,
        mesh=mesh,
        in_specs=placed,
        out_specs=(P("drop", None, None, None, "freq"), P()),
        check_vma=False,
    )
```

```python
import math

import jax
import jax.numpy as jnp
from jax import lax
from jax.experimental import pallas as pl
from jax.experimental.pallas import tpu as pltpu
from jax.sharding import PartitionSpec as P

RX = 32
TX = 4
TAPS = 23
SNRS = 16
FOURIER_POINTS = 4096
DROPS = 32
LANES = 128
NX, NY = 4, 8
NEAR = 4
ALONG_X = ((2, 0), (1, 0), (3, 0))
MESH = pl.DeviceIdType.MESH
F32 = jnp.float32

level_scale = 1.0 / math.sqrt(10.0)


def cos_sin(cycles):
    shifted = cycles + 512
    quadrant = lax.shift_right_logical(shifted, 10) & 3
    x = ((shifted & 1023) - 512).astype(F32) * (2.0 * math.pi / FOURIER_POINTS)
    x2 = x * x
    s = x * (1.0 + x2 * (-1 / 6 + x2 * (1 / 120 + x2 * (-1 / 5040 + x2 * (1 / 362880)))))
    c = 1.0 + x2 * (-0.5 + x2 * (1 / 24 + x2 * (-1 / 720 + x2 * (1 / 40320 + x2 * (-1 / 3628800)))))
    odd = (quadrant & 1) == 1
    cosine = jnp.where(odd, s, c)
    sine = jnp.where(odd, c, s)
    cosine = jnp.where((quadrant == 1) | (quadrant == 2), -cosine, cosine)
    sine = jnp.where(quadrant >= 2, -sine, sine)
    return cosine, sine


def over_sublanes(x):
    x = x + pltpu.roll(x, 4, 0)
    x = x + pltpu.roll(x, 2, 0)
    return x + pltpu.roll(x, 1, 0)


def cmul(a, b):
    return a[0] * b[0] - a[1] * b[1], a[0] * b[1] + a[1] * b[0]


def cmul_conj(a, b):
    return a[0] * b[0] + a[1] * b[1], a[0] * b[1] - a[1] * b[0]


def cadd(a, b):
    return a[0] + b[0], a[1] + b[1]


def halves(x):
    high = x.astype(jnp.bfloat16)
    return high, (x - high.astype(F32)).astype(jnp.bfloat16)


def csub(a, b):
    return a[0] - b[0], a[1] - b[1]


def kernel(
    taps_hbm, lags_hbm, gain_hbm, symbols_hbm, noise_hbm, std_hbm,
    detected_ref, error_ref,
    taps_v, lags_v, gain_v, symbols_v, noise_v, std_v,
    packed, padded, column, gathered, table, channel, noise_f, noise_t, out_f, out_v, row_send, rows, sum_send, sums,
    in_sems, send_sems, recv_sems, y_ready, ready,
):
    n_freq, n_drop = lax.axis_size("freq"), lax.axis_size("drop")
    freq, drop = lax.axis_index("freq"), lax.axis_index("drop")
    barrier = pltpu.get_barrier_semaphore()

    x, y = freq // NY, lax.rem(freq, NY)

    def peer(dx, dy):
        return {"freq": lax.rem(x + dx, NX) * NY + lax.rem(y + dy, NY)}

    def signal(semaphore, device):
        pl.semaphore_signal(semaphore, inc=1, device_id=device, device_id_type=MESH)

    loads = [
        pltpu.make_async_copy(src, dst, in_sems.at[i])
        for i, (src, dst) in enumerate(
            (
                (taps_hbm, taps_v), (lags_hbm, lags_v), (gain_hbm, gain_v),
                (symbols_hbm, symbols_v), (noise_hbm, noise_v), (std_hbm, std_v),
            )
        )
    ]
    for load in loads:
        load.start()

    upper = y // 5
    order = (1 - upper) * (2 * y - 1 + (NY - y) // NY) + upper * 2 * (NY - y)

    def y_at(i):
        odd = lax.rem(i, 2)
        return odd * ((i + 1) // 2) + (1 - odd) * lax.rem(NY - i // 2, NY)

    def y_peer(i):
        return {"freq": x * NY + y_at(i)}

    for dx, dy in ALONG_X:
        signal(barrier, peer(dx, dy))

    @pl.loop(order + 1, NY)
    def _(i):
        signal(barrier, y_peer(i))

    @pl.loop(drop + 1, n_drop)
    def _(i):
        signal(barrier, {"drop": i})

    pl.semaphore_wait(barrier, NX - 1 + order + drop)

    @pl.loop(0, order)
    def _(i):
        signal(y_ready.at[order], y_peer(i))

    padded[...] = jnp.zeros_like(padded)
    loads[0].wait()
    for q in range(4):
        padded[q, :, 0:TAPS] = taps_v[q // 2, q % 2]
    own = padded[0]
    for q in range(1, 4):
        own = own + pltpu.roll(padded[q], 32 * q, 1)
    packed[...] = own
    gathered[y, x] = own

    def copy_to(device, src, dst, i, received=None):
        return pltpu.make_async_remote_copy(
            src_ref=src, dst_ref=dst, send_sem=send_sems.at[i], recv_sem=recv_sems.at[i if received is None else received],
            device_id=device, device_id_type=MESH,
        )

    def all_of(ref, n, i, received=None):
        return copy_to(peer(0, 1), ref.at[pl.ds(0, n)], ref.at[pl.ds(0, n)], i, received)

    for dx, dy in ALONG_X:
        copy_to(peer(dx, dy), packed, gathered.at[y, x], 0).start()

    @pl.loop(0, drop)
    def _(i):
        signal(ready, {"drop": i})


    loads[1].wait()
    loads[2].wait()
    loads[5].wait()
    column[...] = jnp.zeros_like(column)
    column[0:2, 0:TAPS] = lags_v[...].astype(F32)
    column[2:4, 0:SNRS] = std_v[...]
    turned = jnp.transpose(column[...])
    gain = gain_v[...]
    tone = freq * LANES + lax.broadcasted_iota(jnp.int32, (32, LANES), 1)
    table[...] = jnp.zeros_like(table)
    for d in range(2):
        lag = turned[0:32, d : d + 1].astype(jnp.int32)
        cosine, sine = cos_sin((lag * tone) & (FOURIER_POINTS - 1))
        cosine = cosine * gain
        sine = sine * gain
        for at, block in ((0, (cosine, -sine)), (32, (sine, cosine))):
            for c in range(2):
                high, low = halves(block[c])
                lanes = slice(LANES * c, LANES * (c + 1))
                table[d, at : at + 32, lanes] = high
                table[d, at + 64 : at + 96, lanes] = high
                table[d, at + 128 + 64 * d : at + 160 + 64 * d, lanes] = low
    std = [jnp.broadcast_to(turned[0:SNRS, 2 + d : 3 + d], (SNRS, LANES)).reshape(2, 8, LANES) for d in range(2)]

    loads[4].wait()

    @pl.loop(0, 32)
    def _(i):
        at = pl.ds(pl.multiple_of(i * 64, 64), 64)
        noise_f[at, :] = noise_v[at, :].astype(F32)

    @pl.loop(0, RX)
    def _(r):
        for q in range(4):
            levels = noise_f[pl.ds(1024 * (q // 2) + 32 * (q % 2) + r, SNRS, stride=2 * RX), :]
            noise_t[pl.ds(pl.multiple_of(SNRS * (RX * q + r), SNRS), SNRS), :] = levels

    all_of(gathered.at[0], NX - 1, 0).wait_recv()

    def send_row_of_taps(i):
        late = lax.rem(y - y_at(i) + NY + 2, NY) // NEAR
        copy_to(y_peer(i), gathered.at[y], gathered.at[y], 1, 1 + 3 * late).start()

    @pl.loop(0, order)
    def _(i):
        send_row_of_taps(i)

    @pl.loop(order + 1, NY)
    def _(i):
        pl.semaphore_wait(y_ready.at[i], 1)
        send_row_of_taps(i)

    def respond(places):
        rows_of = [gathered[lax.rem(y + 6 + i, NY)].reshape(NX * TX, LANES) for i in places]
        full = jnp.concatenate(rows_of, axis=0)
        high = full.astype(jnp.bfloat16).astype(F32)
        low = pltpu.roll(full - high, 64, 1)
        first = lax.broadcasted_iota(jnp.int32, full.shape, 1) < 64
        at = slice(NX * TX * places[0], NX * TX * (places[-1] + 1))
        for d in range(2):
            mixed = jnp.where(first, high, low) if d == 0 else jnp.where(first, low, high)
            left = jnp.concatenate([mixed, high], axis=1).astype(jnp.bfloat16)
            response = jnp.dot(left, table[d], preferred_element_type=F32)
            for c in range(2):
                channel[2 * d + c, at, :] = response[:, LANES * c : LANES * (c + 1)]

    def gram_terms(groups):
        result = []
        for d in range(2):
            diagonal, upper = [0.0] * TX, {}
            for g in groups:
                h = [[channel[2 * d + c, pl.ds(32 * g + t, 8, stride=TX), :] for c in range(2)] for t in range(TX)]
                for t in range(TX):
                    diagonal[t] = diagonal[t] + h[t][0] * h[t][0] + h[t][1] * h[t][1]
                    for u in range(t + 1, TX):
                        upper[t, u] = cadd(upper.get((t, u), (0.0, 0.0)), cmul_conj(h[t], h[u]))
            result.append((diagonal, upper))
        return result
    def matches(first, last, so_far, unroll):
        result = []
        for d in range(2):

            def step(i, old, d=d):
                r = lax.rem(i, NX) * NY + lax.rem(y + 6 + i // NX, NY)
                noise = [
                    noise_t[pl.ds(pl.multiple_of(SNRS * (RX * (2 * d + c) + r), SNRS), SNRS), :].reshape(2, 8, LANES)
                    for c in range(2)
                ]
                new = []
                for t in range(TX):
                    h = [channel[2 * d + c, pl.ds(TX * i + t, 1), :] for c in range(2)]
                    h = [jnp.broadcast_to(v, (8, LANES))[None] for v in h]
                    new.append(cadd(old[t], cmul_conj(h, noise)))
                return tuple(new)

            result.extend(lax.fori_loop(first, last, step, tuple(so_far[TX * d : TX * (d + 1)]), unroll=unroll))
        return result

    nothing = jnp.zeros((2, 8, LANES), F32)
    all_of(gathered, NEAR - 1, 1).wait_recv()
    respond(range(NEAR))
    early = gram_terms(range(NEAR // 2))
    match = matches(0, NX * NEAR, [(nothing, nothing)] * 8, 8)

    all_of(gathered, NY - NEAR, 1, 4).wait_recv()
    respond(range(NEAR, NY))
    late = gram_terms(range(NEAR // 2, NY // 2))
    match = matches(NX * NEAR, RX, match, True)

    solved, totals, powers = [], [], []
    for d in range(2):
        diagonal = [over_sublanes(early[d][0][t] + late[d][0][t]) for t in range(TX)]
        upper = {at: tuple(over_sublanes(v) for v in cadd(early[d][1][at], late[d][1][at])) for at in early[d][1]}
        powers.append((diagonal[0] + diagonal[1]) + (diagonal[2] + diagonal[3]))
        right = [match[4 * d + t] for t in range(TX)]
        inverse = []
        for i in range(TX):
            inverse.append(1.0 / diagonal[i])
            for j in range(i + 1, TX):
                factor = upper[i, j][0] * inverse[i], -upper[i, j][1] * inverse[i]
                diagonal[j] = diagonal[j] - (factor[0] * upper[i, j][0] - factor[1] * upper[i, j][1])
                for k in range(j + 1, TX):
                    upper[j, k] = csub(upper[j, k], cmul(factor, upper[i, k]))
                right[j] = csub(right[j], cmul(factor, right[i]))
        result = [None] * TX
        for i in reversed(range(TX)):
            partial = right[i]
            for k in range(i + 1, TX):
                partial = csub(partial, cmul(upper[i, k], result[k]))
            result[i] = partial[0] * inverse[i], partial[1] * inverse[i]
        solved.append(result)
        total = result[0][0] * result[0][0] + result[0][1] * result[0][1]
        for t in range(1, TX):
            total = total + result[t][0] * result[t][0] + result[t][1] * result[t][1]
        totals.append(total * (std[d] * std[d]))

    lane8 = lax.broadcasted_iota(jnp.int32, (8, LANES), 1)
    sub8 = lax.broadcasted_iota(jnp.int32, (8, LANES), 0)
    power_rows = jnp.where(sub8 == 0, powers[0], jnp.where(sub8 == 1, powers[1], 0.0))
    stacked = [totals[0][0], totals[0][1], totals[1][0], totals[1][1], power_rows]
    row = jnp.zeros((8, LANES), F32)
    for i, piece in enumerate(stacked):
        row = row + jnp.where(lane8 == sub8 + 8 * i, jnp.sum(piece, axis=1, keepdims=True), 0.0)
    row = jnp.sum(row, axis=0, keepdims=True)
    row_send[...] = row
    rows[freq] = row

    @pl.loop(0, n_freq - 1)
    def _(i):
        far_x, far_y = lax.rem(i, NX), i // NX
        dx = NX // 2 + (far_x + 1) // 2 * (2 * lax.rem(far_x, 2) - 1)
        dy = NY // 2 + (far_y + 1) // 2 * (2 * lax.rem(far_y, 2) - 1)
        copy_to(peer(dx, dy), row_send, rows.at[freq], 2).start()

    loads[3].wait()
    sent = []
    for d in range(2):
        for t in range(TX):
            symbol = symbols_v[pl.ds(64 * d + t, SNRS, stride=TX), :]
            sent.append(
                (
                    (2 * (symbol & 3) - 3).astype(F32) * level_scale,
                    (2 * lax.shift_right_logical(symbol, 2) - 3).astype(F32) * level_scale,
                )
            )

    all_of(rows, n_freq - 1, 2).wait_recv()
    row = jnp.sum(rows[...], axis=0)
    lane = lax.broadcasted_iota(jnp.int32, (1, LANES), 1)
    power = [
        jnp.sum(jnp.where(lane == 32 + d, row, 0.0), axis=1, keepdims=True) * (1.0 / (FOURIER_POINTS * RX * TX))
        for d in range(2)
    ]
    weighted = row * jnp.where(lane < SNRS, power[0], jnp.where(lane < 2 * SNRS, power[1], 0.0))
    sum_send[...] = weighted
    sums[drop] = weighted

    @pl.loop(0, drop)
    def _(i):
        copy_to({"drop": i}, sum_send, sums.at[drop], 3).start()

    @pl.when(drop < n_drop - 1)
    def _():
        pl.semaphore_wait(ready, n_drop - 1 - drop)

    @pl.loop(drop + 1, n_drop)
    def _(i):
        copy_to({"drop": i}, sum_send, sums.at[drop], 3).start()

    for d in range(2):
        amplitude = std[d] * jnp.sqrt(jnp.broadcast_to(power[d], (8, LANES)))
        for t in range(TX):
            for c in range(2):
                estimate = sent[4 * d + t][c] + (amplitude * solved[d][t][c]).reshape(SNRS, LANES)
                out_f[pl.ds(128 * d + 4 * c + t, SNRS, stride=8), :] = estimate
    out_v[...] = out_f[...].astype(jnp.bfloat16)
    store = pltpu.make_async_copy(out_v, detected_ref, in_sems.at[6])
    store.start()

    all_of(sums, n_drop - 1, 3).wait_recv()
    total = jnp.sum(sums[...], axis=0)
    total = total[:, 0:SNRS] + total[:, SNRS : 2 * SNRS]
    error_ref[...] = RX * total / (DROPS * TX * FOURIER_POINTS)

    store.wait()
    all_of(gathered.at[0], NX - 1, 0).wait_send()
    all_of(gathered, NY - 1, 1).wait_send()
    all_of(rows, n_freq - 1, 2).wait_send()
    all_of(sums, n_drop - 1, 3).wait_send()


def write_out(detected_ref, error_ref, detected_out, error_out, sems):
    copies = [
        pltpu.make_async_copy(src, dst, sems.at[i])
        for i, (src, dst) in enumerate(((detected_ref, detected_out), (error_ref, error_out)))
    ]
    for copy in copies:
        copy.start()
    for copy in copies:
        copy.wait()


def shards(taps, echo_lags, front_gain, symbols, noise, noise_std):
    n_freq, n_drop = lax.axis_size("freq"), lax.axis_size("drop")
    vmem = pltpu.VMEM
    detected, error = pl.pallas_call(
        kernel,
        out_shape=(
            jax.ShapeDtypeStruct((2 * SNRS * 8, LANES), jnp.bfloat16),
            jax.ShapeDtypeStruct((1, SNRS), F32),
        ),
        in_specs=[pl.BlockSpec(memory_space=pltpu.HBM)] * 6,
        out_specs=(pl.BlockSpec(memory_space=pl.ANY), pl.BlockSpec(memory_space=pltpu.VMEM)),
        scratch_shapes=[
            vmem((2, 2, TX, TAPS), F32),
            vmem((2, TAPS), jnp.int32),
            vmem((1, LANES), F32),
            vmem((2 * SNRS * TX, LANES), jnp.int32),
            vmem((2 * SNRS * 2 * RX, LANES), jnp.bfloat16),
            vmem((2, SNRS), F32),
            vmem((TX, LANES), F32),
            vmem((4, TX, LANES), F32),
            vmem((LANES, LANES), F32),
            vmem((NY, NX, TX, LANES), F32),
            vmem((2, 2 * LANES, 2 * LANES), jnp.bfloat16),
            vmem((4, RX * TX, LANES), F32),
            vmem((2 * SNRS * 2 * RX, LANES), F32),
            vmem((2 * SNRS * 2 * RX, LANES), F32),
            vmem((2 * SNRS * 8, LANES), F32),
            vmem((2 * SNRS * 8, LANES), jnp.bfloat16),
            vmem((1, LANES), F32),
            vmem((n_freq, 1, LANES), F32),
            vmem((1, LANES), F32),
            vmem((n_drop, 1, LANES), F32),
            pltpu.SemaphoreType.DMA((7,)),
            pltpu.SemaphoreType.DMA((4,)),
            pltpu.SemaphoreType.DMA((5,)),
            pltpu.SemaphoreType.REGULAR((NY,)),
            pltpu.SemaphoreType.REGULAR,
        ],
        compiler_params=pltpu.CompilerParams(collective_id=0, has_side_effects=True, vmem_limit_bytes=16 << 20),
    )(
        *[
            pltpu.with_memory_space_constraint(v, pltpu.HBM)
            for v in (
                jnp.transpose(taps, (0, 1, 3, 2)),
                echo_lags,
                front_gain.reshape(1, LANES),
                symbols.reshape(2 * SNRS * TX, LANES),
                noise.reshape(2 * SNRS * 2 * RX, LANES),
                noise_std,
            )
        ]
    )
    detected, error = pl.pallas_call(
        write_out,
        out_shape=(
            jax.ShapeDtypeStruct((2 * SNRS * 8, LANES), jnp.bfloat16),
            jax.ShapeDtypeStruct((1, SNRS), F32),
        ),
        in_specs=[pl.BlockSpec(memory_space=pltpu.VMEM)] * 2,
        out_specs=[pl.BlockSpec(memory_space=pltpu.HBM)] * 2,
        scratch_shapes=[pltpu.SemaphoreType.DMA((2,))],
        compiler_params=pltpu.CompilerParams(vmem_limit_bytes=1 << 20),
    )(detected, error)
    return detected.reshape(2, SNRS, 2, TX, LANES), error.reshape(SNRS)


def solution(mesh):
    placed = (
        P("drop", None, None, "freq"),
        P("drop", None),
        P("freq"),
        P("drop", None, None, "freq"),
        P("drop", None, None, None, "freq"),
        P("drop", None),
    )
    return jax.shard_map(
        shards,
        mesh=mesh,
        in_specs=placed,
        out_specs=(P("drop", None, None, None, "freq"), P()),
        check_vma=False,
    )
```

```python
import math

import jax
import jax.numpy as jnp
from jax import lax
from jax.experimental import pallas as pl
from jax.experimental.pallas import tpu as pltpu
from jax.sharding import PartitionSpec as P

RX = 32
TX = 4
TAPS = 23
SNRS = 16
FOURIER_POINTS = 4096
DROPS = 32
LANES = 128
NX, NY = 4, 8
NEAR = 4
ALONG_X = ((2, 0), (1, 0), (3, 0))
MESH = pl.DeviceIdType.MESH
F32 = jnp.float32

level_scale = 1.0 / math.sqrt(10.0)


def cos_sin(cycles):
    shifted = cycles + 512
    quadrant = lax.shift_right_logical(shifted, 10) & 3
    x = ((shifted & 1023) - 512).astype(F32) * (2.0 * math.pi / FOURIER_POINTS)
    x2 = x * x
    s = x * (1.0 + x2 * (-1 / 6 + x2 * (1 / 120 + x2 * (-1 / 5040 + x2 * (1 / 362880)))))
    c = 1.0 + x2 * (-0.5 + x2 * (1 / 24 + x2 * (-1 / 720 + x2 * (1 / 40320 + x2 * (-1 / 3628800)))))
    odd = (quadrant & 1) == 1
    cosine = jnp.where(odd, s, c)
    sine = jnp.where(odd, c, s)
    cosine = jnp.where((quadrant == 1) | (quadrant == 2), -cosine, cosine)
    sine = jnp.where(quadrant >= 2, -sine, sine)
    return cosine, sine


def over_sublanes(x):
    x = x + pltpu.roll(x, 4, 0)
    x = x + pltpu.roll(x, 2, 0)
    return x + pltpu.roll(x, 1, 0)


def cmul(a, b):
    return a[0] * b[0] - a[1] * b[1], a[0] * b[1] + a[1] * b[0]


def cmul_conj(a, b):
    return a[0] * b[0] + a[1] * b[1], a[0] * b[1] - a[1] * b[0]


def cadd(a, b):
    return a[0] + b[0], a[1] + b[1]


def halves(x):
    high = x.astype(jnp.bfloat16)
    return high, (x - high.astype(F32)).astype(jnp.bfloat16)


def csub(a, b):
    return a[0] - b[0], a[1] - b[1]


def kernel(
    taps_hbm, lags_hbm, gain_hbm, symbols_hbm, noise_hbm, std_hbm,
    detected_ref, error_ref,
    taps_v, lags_v, gain_v, symbols_v, noise_v, std_v,
    packed, padded, column, gathered, table, channel, noise_f, noise_t, out_f, out_v, row_send, rows, sum_send, sums,
    in_sems, send_sems, recv_sems, y_ready, ready,
):
    n_freq, n_drop = lax.axis_size("freq"), lax.axis_size("drop")
    freq, drop = lax.axis_index("freq"), lax.axis_index("drop")
    barrier = pltpu.get_barrier_semaphore()

    x, y = freq // NY, lax.rem(freq, NY)

    def peer(dx, dy):
        return {"freq": lax.rem(x + dx, NX) * NY + lax.rem(y + dy, NY)}

    def signal(semaphore, device):
        pl.semaphore_signal(semaphore, inc=1, device_id=device, device_id_type=MESH)

    loads = [
        pltpu.make_async_copy(src, dst, in_sems.at[i])
        for i, (src, dst) in enumerate(
            (
                (taps_hbm, taps_v), (lags_hbm, lags_v), (gain_hbm, gain_v),
                (symbols_hbm, symbols_v), (noise_hbm, noise_v), (std_hbm, std_v),
            )
        )
    ]
    for load in loads:
        load.start()

    upper = y // 5
    order = (1 - upper) * (2 * y - 1 + (NY - y) // NY) + upper * 2 * (NY - y)

    def y_at(i):
        odd = lax.rem(i, 2)
        return odd * ((i + 1) // 2) + (1 - odd) * lax.rem(NY - i // 2, NY)

    def y_peer(i):
        return {"freq": x * NY + y_at(i)}

    for dx, dy in ALONG_X:
        signal(barrier, peer(dx, dy))

    @pl.loop(order + 1, NY)
    def _(i):
        signal(barrier, y_peer(i))

    @pl.loop(drop + 1, n_drop)
    def _(i):
        signal(barrier, {"drop": i})

    pl.semaphore_wait(barrier, NX - 1 + order + drop)

    @pl.loop(0, order)
    def _(i):
        signal(y_ready, y_peer(i))

    padded[...] = jnp.zeros_like(padded)
    loads[0].wait()
    for q in range(4):
        padded[q, :, 0:TAPS] = taps_v[q // 2, q % 2]
    own = padded[0]
    for q in range(1, 4):
        own = own + pltpu.roll(padded[q], 32 * q, 1)
    packed[...] = own
    gathered[y, x] = own

    def copy_to(device, src, dst, i, received=None):
        return pltpu.make_async_remote_copy(
            src_ref=src, dst_ref=dst, send_sem=send_sems.at[i], recv_sem=recv_sems.at[i if received is None else received],
            device_id=device, device_id_type=MESH,
        )

    def all_of(ref, n, i, received=None):
        return copy_to(peer(0, 1), ref.at[pl.ds(0, n)], ref.at[pl.ds(0, n)], i, received)

    for dx, dy in ALONG_X:
        copy_to(peer(dx, dy), packed, gathered.at[y, x], 0).start()

    @pl.loop(0, drop)
    def _(i):
        signal(ready, {"drop": i})


    loads[1].wait()
    loads[2].wait()
    loads[5].wait()
    column[...] = jnp.zeros_like(column)
    column[0:2, 0:TAPS] = lags_v[...].astype(F32)
    column[2:4, 0:SNRS] = std_v[...]
    turned = jnp.transpose(column[...])
    gain = gain_v[...]
    tone = freq * LANES + lax.broadcasted_iota(jnp.int32, (32, LANES), 1)
    table[...] = jnp.zeros_like(table)
    for d in range(2):
        lag = turned[0:32, d : d + 1].astype(jnp.int32)
        cosine, sine = cos_sin((lag * tone) & (FOURIER_POINTS - 1))
        cosine = cosine * gain
        sine = sine * gain
        for at, block in ((0, (cosine, -sine)), (32, (sine, cosine))):
            for c in range(2):
                high, low = halves(block[c])
                lanes = slice(LANES * c, LANES * (c + 1))
                table[d, at : at + 32, lanes] = high
                table[d, at + 64 : at + 96, lanes] = high
                table[d, at + 128 + 64 * d : at + 160 + 64 * d, lanes] = low
    std = [jnp.broadcast_to(turned[0:SNRS, 2 + d : 3 + d], (SNRS, LANES)).reshape(2, 8, LANES) for d in range(2)]

    loads[4].wait()

    @pl.loop(0, 32)
    def _(i):
        at = pl.ds(pl.multiple_of(i * 64, 64), 64)
        noise_f[at, :] = noise_v[at, :].astype(F32)

    @pl.loop(0, RX)
    def _(r):
        for q in range(4):
            levels = noise_f[pl.ds(1024 * (q // 2) + 32 * (q % 2) + r, SNRS, stride=2 * RX), :]
            noise_t[pl.ds(pl.multiple_of(SNRS * (RX * q + r), SNRS), SNRS), :] = levels

    all_of(gathered.at[0], NX - 1, 0).wait_recv()

    def send_row_of_taps(i):
        late = lax.rem(y - y_at(i) + NY + 2, NY) // NEAR
        copy_to(y_peer(i), gathered.at[y], gathered.at[y], 1, 1 + 3 * late).start()

    @pl.loop(0, order)
    def _(i):
        send_row_of_taps(i)

    @pl.when(order < NY - 1)
    def _():
        pl.semaphore_wait(y_ready, NY - 1 - order)

    @pl.loop(0, NY - 1 - order)
    def _(i):
        send_row_of_taps(NY - 1 - i)

    def respond(places):
        rows_of = [gathered[lax.rem(y + 6 + i, NY)].reshape(NX * TX, LANES) for i in places]
        full = jnp.concatenate(rows_of, axis=0)
        high = full.astype(jnp.bfloat16).astype(F32)
        low = pltpu.roll(full - high, 64, 1)
        first = lax.broadcasted_iota(jnp.int32, full.shape, 1) < 64
        at = slice(NX * TX * places[0], NX * TX * (places[-1] + 1))
        for d in range(2):
            mixed = jnp.where(first, high, low) if d == 0 else jnp.where(first, low, high)
            left = jnp.concatenate([mixed, high], axis=1).astype(jnp.bfloat16)
            response = jnp.dot(left, table[d], preferred_element_type=F32)
            for c in range(2):
                channel[2 * d + c, at, :] = response[:, LANES * c : LANES * (c + 1)]

    def gram_terms(groups):
        result = []
        for d in range(2):
            diagonal, upper = [0.0] * TX, {}
            for g in groups:
                h = [[channel[2 * d + c, pl.ds(32 * g + t, 8, stride=TX), :] for c in range(2)] for t in range(TX)]
                for t in range(TX):
                    diagonal[t] = diagonal[t] + h[t][0] * h[t][0] + h[t][1] * h[t][1]
                    for u in range(t + 1, TX):
                        upper[t, u] = cadd(upper.get((t, u), (0.0, 0.0)), cmul_conj(h[t], h[u]))
            result.append((diagonal, upper))
        return result
    def matches(first, last, so_far, unroll):
        result = []
        for d in range(2):

            def step(i, old, d=d):
                r = lax.rem(i, NX) * NY + lax.rem(y + 6 + i // NX, NY)
                noise = [
                    noise_t[pl.ds(pl.multiple_of(SNRS * (RX * (2 * d + c) + r), SNRS), SNRS), :].reshape(2, 8, LANES)
                    for c in range(2)
                ]
                new = []
                for t in range(TX):
                    h = [channel[2 * d + c, pl.ds(TX * i + t, 1), :] for c in range(2)]
                    h = [jnp.broadcast_to(v, (8, LANES))[None] for v in h]
                    new.append(cadd(old[t], cmul_conj(h, noise)))
                return tuple(new)

            result.extend(lax.fori_loop(first, last, step, tuple(so_far[TX * d : TX * (d + 1)]), unroll=unroll))
        return result

    nothing = jnp.zeros((2, 8, LANES), F32)
    all_of(gathered, NEAR - 1, 1).wait_recv()
    respond(range(NEAR))
    early = gram_terms(range(NEAR // 2))
    match = matches(0, NX * NEAR, [(nothing, nothing)] * 8, 8)

    all_of(gathered, NY - NEAR, 1, 4).wait_recv()
    respond(range(NEAR, NY))
    late = gram_terms(range(NEAR // 2, NY // 2))
    match = matches(NX * NEAR, RX, match, True)

    solved, totals, powers = [], [], []
    for d in range(2):
        diagonal = [over_sublanes(early[d][0][t] + late[d][0][t]) for t in range(TX)]
        upper = {at: tuple(over_sublanes(v) for v in cadd(early[d][1][at], late[d][1][at])) for at in early[d][1]}
        powers.append((diagonal[0] + diagonal[1]) + (diagonal[2] + diagonal[3]))
        right = [match[4 * d + t] for t in range(TX)]
        inverse = []
        for i in range(TX):
            inverse.append(1.0 / diagonal[i])
            for j in range(i + 1, TX):
                factor = upper[i, j][0] * inverse[i], -upper[i, j][1] * inverse[i]
                diagonal[j] = diagonal[j] - (factor[0] * upper[i, j][0] - factor[1] * upper[i, j][1])
                for k in range(j + 1, TX):
                    upper[j, k] = csub(upper[j, k], cmul(factor, upper[i, k]))
                right[j] = csub(right[j], cmul(factor, right[i]))
        result = [None] * TX
        for i in reversed(range(TX)):
            partial = right[i]
            for k in range(i + 1, TX):
                partial = csub(partial, cmul(upper[i, k], result[k]))
            result[i] = partial[0] * inverse[i], partial[1] * inverse[i]
        solved.append(result)
        total = result[0][0] * result[0][0] + result[0][1] * result[0][1]
        for t in range(1, TX):
            total = total + result[t][0] * result[t][0] + result[t][1] * result[t][1]
        totals.append(total * (std[d] * std[d]))

    lane8 = lax.broadcasted_iota(jnp.int32, (8, LANES), 1)
    sub8 = lax.broadcasted_iota(jnp.int32, (8, LANES), 0)
    stacked = [totals[0][0], totals[0][1], totals[1][0], totals[1][1]]
    row = jnp.zeros((8, LANES), F32)
    for i, piece in enumerate(stacked):
        row = row + jnp.where(lane8 == sub8 + 8 * i, jnp.sum(piece, axis=1, keepdims=True), 0.0)
    row = jnp.sum(row, axis=0, keepdims=True)
    part = [jnp.sum(powers[d][0:1], axis=1, keepdims=True) for d in range(2)]
    row = jnp.concatenate([row, jnp.where(lane8[0:1] < SNRS, part[0], part[1])], axis=0)
    row_send[...] = row
    rows[freq] = row

    @pl.loop(0, n_freq - 1)
    def _(i):
        far_x, far_y = lax.rem(i, NX), i // NX
        dx = NX // 2 + (far_x + 1) // 2 * (2 * lax.rem(far_x, 2) - 1)
        dy = NY // 2 + (far_y + 1) // 2 * (2 * lax.rem(far_y, 2) - 1)
        copy_to(peer(dx, dy), row_send, rows.at[freq], 2).start()

    loads[3].wait()
    sent = []
    for d in range(2):
        for t in range(TX):
            symbol = symbols_v[pl.ds(64 * d + t, SNRS, stride=TX), :]
            sent.append(
                (
                    (2 * (symbol & 3) - 3).astype(F32) * level_scale,
                    (2 * lax.shift_right_logical(symbol, 2) - 3).astype(F32) * level_scale,
                )
            )

    all_of(rows, n_freq - 1, 2).wait_recv()
    row = jnp.sum(rows[...], axis=0)
    powers_row = row[1:2] * (1.0 / (FOURIER_POINTS * RX * TX))
    weighted = row[0:1] * powers_row
    sum_send[...] = weighted
    sums[drop] = weighted

    @pl.loop(0, drop)
    def _(i):
        copy_to({"drop": i}, sum_send, sums.at[drop], 3).start()

    @pl.when(drop < n_drop - 1)
    def _():
        pl.semaphore_wait(ready, n_drop - 1 - drop)

    @pl.loop(drop + 1, n_drop)
    def _(i):
        copy_to({"drop": i}, sum_send, sums.at[drop], 3).start()

    lane = lax.broadcasted_iota(jnp.int32, (1, LANES), 1)
    power = [jnp.sum(jnp.where(lane == SNRS * d, powers_row, 0.0), axis=1, keepdims=True) for d in range(2)]
    for d in range(2):
        amplitude = std[d] * jnp.sqrt(jnp.broadcast_to(power[d], (8, LANES)))
        for t in range(TX):
            for c in range(2):
                estimate = sent[4 * d + t][c] + (amplitude * solved[d][t][c]).reshape(SNRS, LANES)
                out_f[pl.ds(128 * d + 4 * c + t, SNRS, stride=8), :] = estimate
    out_v[...] = out_f[...].astype(jnp.bfloat16)
    store = pltpu.make_async_copy(out_v, detected_ref, in_sems.at[6])
    store.start()

    all_of(sums, n_drop - 1, 3).wait_recv()
    total = jnp.sum(sums[...], axis=0)
    total = total[:, 0:SNRS] + total[:, SNRS : 2 * SNRS]
    error_ref[...] = RX * total / (DROPS * TX * FOURIER_POINTS)

    store.wait()
    all_of(gathered.at[0], NX - 1, 0).wait_send()
    all_of(gathered, NY - 1, 1).wait_send()
    all_of(rows, n_freq - 1, 2).wait_send()
    all_of(sums, n_drop - 1, 3).wait_send()


def write_out(detected_ref, error_ref, detected_out, error_out, sems):
    copies = [
        pltpu.make_async_copy(src, dst, sems.at[i])
        for i, (src, dst) in enumerate(((detected_ref, detected_out), (error_ref, error_out)))
    ]
    for copy in copies:
        copy.start()
    for copy in copies:
        copy.wait()


def shards(taps, echo_lags, front_gain, symbols, noise, noise_std):
    n_freq, n_drop = lax.axis_size("freq"), lax.axis_size("drop")
    vmem = pltpu.VMEM
    detected, error = pl.pallas_call(
        kernel,
        out_shape=(
            jax.ShapeDtypeStruct((2 * SNRS * 8, LANES), jnp.bfloat16),
            jax.ShapeDtypeStruct((1, SNRS), F32),
        ),
        in_specs=[pl.BlockSpec(memory_space=pltpu.HBM)] * 6,
        out_specs=(pl.BlockSpec(memory_space=pl.ANY), pl.BlockSpec(memory_space=pltpu.VMEM)),
        scratch_shapes=[
            vmem((2, 2, TX, TAPS), F32),
            vmem((2, TAPS), jnp.int32),
            vmem((1, LANES), F32),
            vmem((2 * SNRS * TX, LANES), jnp.int32),
            vmem((2 * SNRS * 2 * RX, LANES), jnp.bfloat16),
            vmem((2, SNRS), F32),
            vmem((TX, LANES), F32),
            vmem((4, TX, LANES), F32),
            vmem((LANES, LANES), F32),
            vmem((NY, NX, TX, LANES), F32),
            vmem((2, 2 * LANES, 2 * LANES), jnp.bfloat16),
            vmem((4, RX * TX, LANES), F32),
            vmem((2 * SNRS * 2 * RX, LANES), F32),
            vmem((2 * SNRS * 2 * RX, LANES), F32),
            vmem((2 * SNRS * 8, LANES), F32),
            vmem((2 * SNRS * 8, LANES), jnp.bfloat16),
            vmem((2, LANES), F32),
            vmem((n_freq, 2, LANES), F32),
            vmem((1, LANES), F32),
            vmem((n_drop, 1, LANES), F32),
            pltpu.SemaphoreType.DMA((7,)),
            pltpu.SemaphoreType.DMA((4,)),
            pltpu.SemaphoreType.DMA((5,)),
            pltpu.SemaphoreType.REGULAR,
            pltpu.SemaphoreType.REGULAR,
        ],
        compiler_params=pltpu.CompilerParams(collective_id=0, has_side_effects=True, vmem_limit_bytes=16 << 20),
    )(
        *[
            pltpu.with_memory_space_constraint(v, pltpu.HBM)
            for v in (
                jnp.transpose(taps, (0, 1, 3, 2)),
                echo_lags,
                front_gain.reshape(1, LANES),
                symbols.reshape(2 * SNRS * TX, LANES),
                noise.reshape(2 * SNRS * 2 * RX, LANES),
                noise_std,
            )
        ]
    )
    detected, error = pl.pallas_call(
        write_out,
        out_shape=(
            jax.ShapeDtypeStruct((2 * SNRS * 8, LANES), jnp.bfloat16),
            jax.ShapeDtypeStruct((1, SNRS), F32),
        ),
        in_specs=[pl.BlockSpec(memory_space=pltpu.VMEM)] * 2,
        out_specs=[pl.BlockSpec(memory_space=pltpu.HBM)] * 2,
        scratch_shapes=[pltpu.SemaphoreType.DMA((2,))],
        compiler_params=pltpu.CompilerParams(vmem_limit_bytes=1 << 20),
    )(detected, error)
    return detected.reshape(2, SNRS, 2, TX, LANES), error.reshape(SNRS)


def solution(mesh):
    placed = (
        P("drop", None, None, "freq"),
        P("drop", None),
        P("freq"),
        P("drop", None, None, "freq"),
        P("drop", None, None, None, "freq"),
        P("drop", None),
    )
    return jax.shard_map(
        shards,
        mesh=mesh,
        in_specs=placed,
        out_specs=(P("drop", None, None, None, "freq"), P()),
        check_vma=False,
    )
```
